32 devices in a mesh: cell: 16 (over z, y, core), dir: 2 (over x).
Axes of the slice: x: 2, y: 2, z: 4, core: 2. Of those that a mesh axis runs over, the one named last changes fastest.
Arguments:
- atom_features: bfloat16 [512, 128, 128], P('cell'), may hold values from -6 to 6
- positions: bfloat16 [512, 3, 128], P('cell'), may hold values from 0 to 12
- neighbours: int32 [512, 4], P('cell'), may hold values from 0 to 39, as said below
- counts: int32 [16], replicated, may hold values from 4 to 28, as said below
- filter_gains: float32 [8, 128], replicated, may hold values from -0.25 to 0.25
- w_update: bfloat16 [128, 128], replicated, may hold values from -0.5 to 0.5
- projections: bfloat16 [128, 384], replicated, may hold values from -0.5 to 0.5
- w_output: bfloat16 [128, 128], replicated, may hold values from -0.5 to 0.5
Outputs:
- attended: bfloat16 [256, 128, 128], P(('cell', 'dir'))
The draws below stay inside these ranges and needn't reach their ends.
Inputs may be any that keep to these rules, and one draw needn't show every extreme that they name: counts[c] live slots (slots 0 to counts[c] - 1) in cell c; the counts sum to 256; some cell holds the least and some the most. `neighbours`: for a live slot of cell c every entry is below 4 (a face block of the cell before), or from 4 to 4 + counts[c] - 1 (a live block of c), or 36 or more (a face block of the cell after); entries of dead slots lie in the same range.
All inputs are finite; a program needn't handle non-finite values.
Results may differ from the reference program's by a relative error of at most 0.014.
Values may be sent and summed in bfloat16 or wider, within the bound.
A program may use at most 128 MiB of HBM per device.

```python
import math
import jax
import jax.numpy as jnp
from jax import lax

F = 128
DIRS = 50
NRBF = 8
BLK = 128
NNB = 4
H = 4
EQ = 16
CAPB = 32
KSLOT = 2
NATOMS = 32768
N_CELL = 16


def cell_counts(key):
    folded = jax.random.fold_in(key, 101)
    first_key, second_key = jax.random.split(folded)
    surplus = jax.random.randint(first_key, (N_CELL,), 0, EQ - H + 1)
    summit_cell = jax.random.randint(second_key, (), 0, N_CELL)
    cell_order = jnp.arange(N_CELL)
    surplus = jnp.where(cell_order == summit_cell, EQ - H, surplus)
    surplus = jnp.where(cell_order == (summit_cell - 1) % N_CELL, 0, surplus)
    surplus = jnp.where(cell_order == (summit_cell + 1) % N_CELL, 0, surplus)
    return (EQ + surplus - jnp.roll(surplus, 1)).astype(jnp.int32)


def draw_counts(key, part):
    return cell_counts(key)


def draw_neighbours(key, part):
    live_count = jnp.repeat(cell_counts(key), CAPB, total_repeat_length=N_CELL * CAPB)[:, None]
    chosen_key = jax.random.fold_in(key, 202)
    chosen = jax.random.randint(chosen_key, (N_CELL * CAPB, NNB), 0, live_count + 2 * H)
    entries = jnp.where(chosen < H + live_count, chosen, chosen - live_count + CAPB)
    slot_order = (jnp.arange(N_CELL * CAPB) % CAPB)[:, None]
    column_order = jnp.arange(NNB)[None, :]
    entries = jnp.where((slot_order == 0) & (column_order == 0), 0, entries)
    entries = jnp.where((slot_order == 0) & (column_order == 1), 2 * H + CAPB - 1, entries)
    return entries.astype(jnp.int32)


def shard_levels(own_key, dims, pieces, low, top_value):
    factor_of = 1.0
    for axis_at, blocks in pieces:
        steps = jax.random.uniform(jax.random.fold_in(jax.random.fold_in(own_key, 6), axis_at), (blocks,), jnp.float32, low / len(pieces), top_value / len(pieces))
        factor_of = factor_of * jnp.repeat(jnp.exp(steps), dims[axis_at] // blocks).reshape((-1,) + (1,) * (len(dims) - 1 - axis_at))
    return factor_of


def bell_draw(key, dims, scale, bound, cuts=(), kind=jnp.bfloat16):
    loudness = shard_levels(key, dims, cuts, -0.22, 0.18) if cuts else 1.0
    values = jax.random.normal(key, dims, jnp.float32) * scale * loudness
    return jnp.minimum(jnp.maximum(values, -bound), bound).astype(kind)


def setup_inputs(seed: int = 0) -> dict:
    keys = jax.random.split(jax.random.key(seed), 9)
    return {
        "atom_features": bell_draw(keys[0], (N_CELL * CAPB, BLK, F), 1.0, 6.0, ((0, 16),)),
        "positions": jnp.clip(12.0 * jax.random.uniform(keys[1], (N_CELL * CAPB, 3, BLK), jnp.float32) ** shard_levels(keys[1], (N_CELL * CAPB, 3, BLK), ((0, 16),), -0.2, 0.2), 0.0, 12.0).astype(jnp.bfloat16),
        "neighbours": draw_neighbours(jax.random.fold_in(keys[8], 71), 0),
        "counts": draw_counts(jax.random.fold_in(keys[8], 71), 0),
        "filter_gains": bell_draw(keys[4], (NRBF, F), (NNB * BLK) ** -0.5, 0.25, (), jnp.float32),
        "w_update": bell_draw(keys[5], (F, F), F ** -0.5, 0.5),
        "projections": bell_draw(keys[6], (F, 3 * F), F ** -0.5, 0.5),
        "w_output": bell_draw(keys[7], (F, F), F ** -0.5, 0.5),
    }


slab_width = 12.0
radial_width = 0.6
golden_turn = math.pi * (3.0 - math.sqrt(5.0))

def shift_component(positions_in, amount):
    marker = (jnp.arange(positions_in.shape[-2]) == 0).astype(jnp.float32)
    return positions_in + amount * marker[:, None]

def direction_table(total):
    dir_order = jnp.arange(total, dtype=jnp.float32)
    height = 1.0 - (2.0 * dir_order + 1.0) / total
    radius = jnp.sqrt(1.0 - height * height)
    turning = dir_order * golden_turn
    return jnp.stack([radius * jnp.cos(turning), radius * jnp.sin(turning), height], axis=1)

def frequency_table(width):
    half_width = width // 2
    base_part = 0.5 * (jnp.arange(half_width, dtype=jnp.float32) + 1.0) / half_width
    return jnp.concatenate([base_part, base_part])

def phases(coords, directions, frequencies):
    projected = directions[:, 0:1] * coords[0][None] + directions[:, 1:2] * coords[1][None] + directions[:, 2:3] * coords[2][None]
    return projected[:, :, None] * frequencies

def rotate(values, angle):
    half_width = values.shape[-1] // 2
    swapped = jnp.concatenate([-values[:, half_width:], values[:, :half_width]], axis=-1)
    return (values[None] * jnp.cos(angle) + swapped[None] * jnp.sin(angle)).astype(jnp.bfloat16)

def radial_message(own_positions, near_positions, near_features, filter_gains):
    differ = own_positions[None, :, :, None] - near_positions[:, :, None, :]
    distance = jnp.sqrt(lax.optimization_barrier(jnp.sum(differ * differ, axis=1)))
    centers = 2.0 + 2.0 * jnp.arange(filter_gains.shape[0], dtype=jnp.float32)
    scaled = (distance[:, None] - centers[None, :, None, None]) / radial_width
    radial = jnp.exp(-scaled * scaled).astype(jnp.bfloat16)
    summed = jnp.einsum('nkab,nbf->kaf', radial.astype(jnp.float32), near_features.astype(jnp.float32))
    return lax.optimization_barrier(jnp.sum(summed * filter_gains[:, None, :], axis=0))

def reference(atom_features, positions, neighbours, counts, filter_gains, w_update, projections, w_output):
    count_ends = jnp.cumsum(counts).astype(jnp.int32)
    starts = count_ends - counts
    target = jnp.arange(N_CELL * EQ, dtype=jnp.int32)
    owner = target // EQ
    local_row = target % EQ
    global_index = (local_row // KSLOT * N_CELL + owner) * KSLOT + local_row % KSLOT
    source = lax.optimization_barrier(jnp.sum((count_ends[None, :] <= global_index[:, None]).astype(jnp.int32), axis=1)).astype(jnp.int32)
    slot_ids = (source * CAPB + (global_index - starts[source])).astype(jnp.int32)

    def one_block(slot_id, cell_id):
        entries = neighbours[slot_id]
        lower = entries < H
        upper = entries >= H + CAPB
        near_cell = jnp.where(lower, (cell_id - 1) % N_CELL, jnp.where(upper, (cell_id + 1) % N_CELL, cell_id))
        near_slot = jnp.where(lower, entries, jnp.where(upper, entries - H - CAPB, entries - H))
        amount = jnp.where(lower, -slab_width, jnp.where(upper, slab_width, 0.0))
        near_rows = (near_cell * CAPB + near_slot).astype(jnp.int32)
        near_positions = shift_component(positions[near_rows].astype(jnp.float32), amount[:, None, None])
        own_positions = positions[slot_id].astype(jnp.float32)
        message = radial_message(own_positions, near_positions, atom_features[near_rows], filter_gains)
        activated = jax.nn.silu(message).astype(jnp.bfloat16)
        updated = atom_features[slot_id].astype(jnp.float32) + jnp.dot(activated, w_update, preferred_element_type=jnp.float32)
        moved = shift_component(own_positions, slab_width * cell_id.astype(jnp.float32))
        return (updated.astype(jnp.bfloat16), moved)
    batch_width = math.gcd(32, N_CELL * EQ)
    batched = lax.map(lambda paired: jax.vmap(one_block)(paired[0], paired[1]), (slot_ids.reshape(-1, batch_width), source.reshape(-1, batch_width)))
    balanced_features = batched[0].reshape(-1, BLK, F)
    balanced_positions = batched[1].reshape(-1, 3, BLK)
    flat = balanced_features.reshape(-1, F)
    qkv = jnp.dot(flat, projections, preferred_element_type=jnp.float32)
    queries = qkv[:, :F]
    keys_rows = qkv[:, F:2 * F]
    values = qkv[:, 2 * F:].astype(jnp.bfloat16)
    coords = jnp.transpose(balanced_positions, (1, 0, 2)).reshape(3, -1)
    dir_table = direction_table(DIRS)
    frequencies = frequency_table(F)

    def one_state(direction):
        key_rot = rotate(keys_rows, phases(coords, direction[None], frequencies))[0]
        return jnp.dot(key_rot.T, values, preferred_element_type=jnp.float32)
    states = lax.map(one_state, dir_table).astype(jnp.bfloat16)

    def add_direction(running, paired):
        direction, state = paired
        query_rot = rotate(queries, phases(coords, direction[None], frequencies))[0]
        return (running + jnp.dot(query_rot, state, preferred_element_type=jnp.float32), None)
    running, unused = lax.scan(add_direction, jnp.zeros((queries.shape[0], F), jnp.float32), (dir_table, states))
    mix_scale = 1.0 / math.sqrt(DIRS * NATOMS * F)
    mixed = (running * mix_scale).astype(jnp.bfloat16)
    attended = jnp.dot(mixed, w_output, preferred_element_type=jnp.float32).astype(jnp.bfloat16)
    return attended.reshape(N_CELL * EQ, BLK, F)
```

```python
import functools
import math

import jax
import jax.numpy as jnp
import numpy as np
from jax import lax
from jax.experimental import pallas as pl
from jax.experimental.pallas import tpu as pltpu
from jax.sharding import PartitionSpec as P

DIRS = 50
H = 4


slab_width = 12.0
radial_width = 0.6
golden_turn = math.pi * (3.0 - math.sqrt(5.0))


def extended(cells, sides, width):
    for axis, dim in sides:
        count = lax.axis_size(axis)
        head = lax.slice_in_dim(cells, 0, width, axis=dim)
        tail = lax.slice_in_dim(cells, cells.shape[dim] - width, cells.shape[dim], axis=dim)
        cells = jnp.concatenate(
            [
                lax.ppermute(tail, axis, [(i, (i + 1) % count) for i in range(count)]),
                cells,
                lax.ppermute(head, axis, [((i + 1) % count, i) for i in range(count)]),
            ],
            axis=dim,
        )
    return cells


def shift_component(positions_in, amount):
    marker = (jnp.arange(positions_in.shape[-2]) == 0).astype(jnp.float32)
    return positions_in + amount * marker[:, None]


def direction_rows(total):
    order = np.arange(total, dtype=np.float64)
    height = 1.0 - (2.0 * order + 1.0) / total
    radius = np.sqrt(1.0 - height * height)
    turning = order * golden_turn
    padded = -(-total // 8) * 8
    table = np.zeros((padded, 128), np.float32)
    table[:total, 0] = radius * np.cos(turning)
    table[:total, 1] = radius * np.sin(turning)
    table[:total, 2] = height
    table[:total, 3] = 1.0
    return table


def rotated_groups(table, coords, source, half, group, emit):
    base = (
        table[:, 0:1] * coords[0:1] + table[:, 1:2] * coords[1:2] + table[:, 2:3] * coords[2:3]
    ) * (0.5 / half)
    alive = jnp.broadcast_to(table[:, 3:4], base.shape)
    c1, s1 = jnp.cos(base), jnp.sin(base)
    c2, s2 = c1 * c1 - s1 * s1, 2.0 * (s1 * c1)
    c3, s3 = c2 * c1 - s2 * s1, s2 * c1 + c2 * s1
    c4, s4 = c2 * c2 - s2 * s2, 2.0 * (s2 * c2)
    step = 2.0 * c4
    c1, s1, c2, s2, c3, s3, c4, s4 = [v * alive for v in (c1, s1, c2, s2, c3, s3, c4, s4)]
    zero = jnp.zeros_like(alive)
    older = [(c3, -s3), (c2, -s2), (c1, -s1), (alive, zero)]
    newer = [(c1, s1), (c2, s2), (c3, s3), (c4, s4)]
    for first in range(0, half, group):
        low, high = [], []
        for p in range(first, first + group):
            if p >= 4:
                lane = p % 4
                cosine = step * newer[lane][0] - older[lane][0]
                sine = step * newer[lane][1] - older[lane][1]
                older[lane] = newer[lane]
                newer[lane] = (cosine, sine)
            cosine, sine = newer[p % 4]
            a = source(p)
            b = source(p + half)
            low.append(a * cosine - b * sine)
            high.append(b * cosine + a * sine)
        emit(first // group, jnp.concatenate(low + high, axis=0).astype(jnp.bfloat16))


def kv_kernel(group, chunk, table_ref, coords_ref, rows_ref, weights_t_ref, weights_ref, states_ref, keys, values):
    width = rows_ref.shape[1]
    half = width // 2
    atoms = rows_ref.shape[0]

    @pl.when(pl.program_id(0) == 0)
    def _():
        keys[...] = lax.dot_general(
            weights_t_ref[width : 2 * width, :], rows_ref[...], (((1,), (1,)), ((), ())),
            preferred_element_type=jnp.float32,
        )
        values[...] = jnp.dot(
            rows_ref[...], weights_ref[:, 2 * width :], preferred_element_type=jnp.float32
        ).astype(jnp.bfloat16)

    states_ref[...] = jnp.zeros_like(states_ref)
    size = group * 16

    def advance(turn, carried):
        at = pl.ds(pl.multiple_of(turn * chunk, chunk), chunk)
        value_rows = values[at, :]

        def emit(index, turned):
            states_ref[0, index * size : (index + 1) * size, :] += jnp.dot(
                turned, value_rows, preferred_element_type=jnp.float32
            )

        rotated_groups(
            table_ref[...], coords_ref[:, at],
            lambda p: jnp.broadcast_to(keys[p : p + 1, at], (8, chunk)), half, group, emit,
        )
        return carried

    lax.fori_loop(0, atoms // chunk, advance, 0)


def query_kernel(group, chunk, scale, table_ref, coords_ref, rows_ref, weights_t_ref, output_ref, states_ref, out_ref, queries, total):
    width = rows_ref.shape[1]
    half = width // 2
    atoms = rows_ref.shape[0]

    @pl.when(pl.program_id(0) == 0)
    def _():
        queries[...] = lax.dot_general(
            weights_t_ref[:width, :], rows_ref[...], (((1,), (1,)), ((), ())),
            preferred_element_type=jnp.float32,
        )
        total[...] = jnp.zeros_like(total)

    size = group * 16
    flipped = states_ref[0].T

    def advance(turn, carried):
        at = pl.ds(pl.multiple_of(turn * chunk, chunk), chunk)
        parts = []

        def emit(index, turned):
            parts.append(
                jnp.dot(
                    flipped[:, index * size : (index + 1) * size], turned,
                    preferred_element_type=jnp.float32,
                )
            )

        rotated_groups(
            table_ref[...], coords_ref[:, at],
            lambda p: jnp.broadcast_to(queries[p : p + 1, at], (8, chunk)), half, group, emit,
        )
        total[:, at] += sum(parts[1:], parts[0])
        return carried

    lax.fori_loop(0, atoms // chunk, advance, 0)

    @pl.when(pl.program_id(0) == pl.num_programs(0) - 1)
    def _():
        mixed = (total[...] * scale).T.astype(jnp.bfloat16)
        out_ref[...] = jnp.dot(
            mixed, output_ref[...], preferred_element_type=jnp.float32
        ).astype(jnp.bfloat16)


def whole(shape):
    return pl.BlockSpec(shape, lambda i: (0,) * len(shape))


def kv_states(table, coords, flat, weights_t, weights):
    atoms, width = flat.shape
    groups = table.shape[0] // 8
    chunk = min(256, atoms)
    group = 16
    return pl.pallas_call(
        functools.partial(kv_kernel, group, chunk),
        grid=(groups,),
        out_shape=jax.ShapeDtypeStruct((groups, width * 8, width), jnp.float32),
        in_specs=[
            pl.BlockSpec((8, 128), lambda i: (i, 0)),
            whole(coords.shape),
            whole(flat.shape),
            whole(weights_t.shape),
            whole(weights.shape),
        ],
        out_specs=pl.BlockSpec((1, width * 8, width), lambda i: (i, 0, 0)),
        scratch_shapes=[pltpu.VMEM((width, atoms), jnp.float32), pltpu.VMEM((atoms, width), jnp.bfloat16)],
        name="kv_states",
    )(table, coords, flat, weights_t, weights)


def query_mix(table, coords, flat, weights_t, w_output, states, scale):
    atoms, width = flat.shape
    groups = table.shape[0] // 8
    chunk = min(256, atoms)
    group = 16
    return pl.pallas_call(
        functools.partial(query_kernel, group, chunk, scale),
        grid=(groups,),
        out_shape=jax.ShapeDtypeStruct((atoms, width), jnp.bfloat16),
        in_specs=[
            pl.BlockSpec((8, 128), lambda i: (i, 0)),
            whole(coords.shape),
            whole(flat.shape),
            whole(weights_t.shape),
            whole(w_output.shape),
            pl.BlockSpec((1, width * 8, width), lambda i: (i, 0, 0)),
        ],
        out_specs=whole((atoms, width)),
        scratch_shapes=[pltpu.VMEM((width, atoms), jnp.float32), pltpu.VMEM((width, atoms), jnp.float32)],
        name="query_mix",
    )(table, coords, flat, weights_t, w_output, states)


def radial_terms(own_positions, near_positions, near_features, filter_gains):
    differ = own_positions[:, None, :, :, None] - near_positions[:, :, :, None, :]
    distance = jnp.sqrt(jnp.sum(differ * differ, axis=2))
    centers = 2.0 + 2.0 * jnp.arange(filter_gains.shape[0], dtype=jnp.float32)
    scaled = (distance[:, :, None] - centers[None, None, :, None, None]) / radial_width
    radial = jnp.exp(-scaled * scaled).astype(jnp.bfloat16)
    summed = jnp.einsum(
        "gnkab,gnbf->gkaf", radial, near_features, preferred_element_type=jnp.float32
    )
    return jnp.sum(summed * filter_gains[None, :, None, :], axis=1)


def block_messages(
    first_slot,
    live_count,
    slot_count,
    group_width,
    neighbours,
    extended_features,
    extended_positions,
    filter_gains,
    face_blocks,
):
    initial = jnp.zeros(
        (slot_count, extended_features.shape[1], extended_features.shape[2]), jnp.float32
    )

    def block_advance(turn_index, running):
        start_slot = first_slot + turn_index * group_width
        picked = lax.dynamic_slice_in_dim(neighbours, start_slot, group_width, 0)
        near_features = extended_features[picked]
        near_positions = extended_positions[picked]
        own_positions = lax.dynamic_slice_in_dim(
            extended_positions, start_slot + face_blocks, group_width, 0
        )
        result = radial_terms(own_positions, near_positions, near_features, filter_gains)
        return lax.dynamic_update_slice_in_dim(running, result, turn_index * group_width, 0)

    group_total = (live_count + group_width - 1) // group_width
    return lax.fori_loop(0, group_total, block_advance, initial)


def per_device(
    atom_features, positions, neighbours, counts, filter_gains, w_update, projections, w_output
):
    cells = lax.axis_size("cell")
    cell_index = lax.axis_index("cell")
    dirs_count = lax.axis_size("dir")
    dir_index = lax.axis_index("dir")
    capacity, block_atoms, width = atom_features.shape
    balanced_blocks = capacity // 2
    face_blocks = H
    faces_features, faces_positions = (
        extended(atom_features[:face_blocks], (("cell", 0),), face_blocks),
        extended(positions[:face_blocks], (("cell", 0),), face_blocks),
    )
    float_positions = positions.astype(jnp.float32)
    faces_float = faces_positions.astype(jnp.float32)
    extended_features = jnp.concatenate(
        [faces_features[:face_blocks], atom_features, faces_features[2 * face_blocks :]], axis=0
    )
    extended_positions = jnp.concatenate(
        [
            shift_component(faces_float[:face_blocks], -slab_width),
            float_positions,
            shift_component(faces_float[2 * face_blocks :], slab_width),
        ],
        axis=0,
    )
    own_count = counts[cell_index]
    share_slots = capacity // dirs_count
    first_slot = dir_index * share_slots
    live_count = jnp.clip(own_count - first_slot, 0, share_slots)
    message = block_messages(
        first_slot,
        live_count,
        share_slots,
        2,
        neighbours,
        extended_features,
        extended_positions,
        filter_gains,
        face_blocks,
    )
    own_features = lax.dynamic_slice_in_dim(atom_features, first_slot, share_slots, 0)
    activated = jax.nn.silu(message).astype(jnp.bfloat16)
    updated_share = (
        own_features.astype(jnp.float32)
        + jnp.dot(activated, w_update, preferred_element_type=jnp.float32)
    ).astype(jnp.bfloat16)
    updated = lax.all_gather(updated_share, "dir", axis=0, tiled=True)
    count_ends = jnp.cumsum(counts)
    starts = count_ends - counts
    first_live = starts[cell_index]
    slot_cap = max(1, 2 * balanced_blocks // cells)
    period = cells * slot_cap
    slot_order = jnp.arange(period, dtype=jnp.int32)
    offset = (slot_order - first_live) % period
    is_live = offset < own_count
    rows_picked = jnp.where(is_live, offset, 0)
    send_features = jnp.where(
        is_live[:, None, None], updated[rows_picked], jnp.zeros((), jnp.bfloat16)
    )
    send_positions = jnp.where(
        is_live[:, None, None], positions[rows_picked], jnp.zeros((), jnp.bfloat16)
    )
    received_features, received_positions = (
        lax.all_to_all(send_features, "cell", split_axis=0, concat_axis=0, tiled=True),
        lax.all_to_all(send_positions, "cell", split_axis=0, concat_axis=0, tiled=True),
    )
    target = jnp.arange(balanced_blocks, dtype=jnp.int32)
    within = target % slot_cap
    global_index = (target // slot_cap * cells + cell_index) * slot_cap + within
    source = jnp.sum((count_ends[None, :] <= global_index[:, None]).astype(jnp.int32), axis=1)
    pick_rows = source * slot_cap + within
    balanced_features = received_features[pick_rows]
    balanced_positions = shift_component(
        received_positions[pick_rows].astype(jnp.float32),
        slab_width * source.astype(jnp.float32)[:, None, None],
    )
    share_blocks = balanced_blocks // dirs_count
    rows_features = lax.dynamic_slice_in_dim(
        balanced_features, dir_index * share_blocks, share_blocks, 0
    )
    rows_positions = lax.dynamic_slice_in_dim(
        balanced_positions, dir_index * share_blocks, share_blocks, 0
    )
    flat = rows_features.reshape(-1, width)
    coords = jnp.transpose(rows_positions, (1, 0, 2)).reshape(3, -1)
    table = jnp.asarray(direction_rows(DIRS))
    weights_t = projections.T
    local_states = kv_states(table, coords, flat, weights_t, projections)
    states = lax.psum(local_states, ("cell", "dir")).astype(jnp.bfloat16)
    mix_scale = 1.0 / math.sqrt(DIRS * cells * balanced_blocks * block_atoms * width)
    attended = query_mix(table, coords, flat, weights_t, w_output, states, mix_scale)
    return attended.reshape(-1, block_atoms, width)


def solution(mesh):
    placed = (
        P("cell", None, None),
        P("cell", None, None),
        P("cell", None),
        P(),
        P(),
        P(),
        P(),
        P(),
    )
    return jax.shard_map(
        per_device,
        mesh=mesh,
        in_specs=placed,
        out_specs=P(("cell", "dir"), None, None),
        check_vma=False,
    )
```

```python
import functools
import math

import jax
import jax.numpy as jnp
import numpy as np
from jax import lax
from jax.experimental import pallas as pl
from jax.experimental.pallas import tpu as pltpu
from jax.sharding import PartitionSpec as P

DIRS = 50
H = 4


slab_width = 12.0
radial_width = 0.6
golden_turn = math.pi * (3.0 - math.sqrt(5.0))


def extended(cells, sides, width):
    for axis, dim in sides:
        count = lax.axis_size(axis)
        head = lax.slice_in_dim(cells, 0, width, axis=dim)
        tail = lax.slice_in_dim(cells, cells.shape[dim] - width, cells.shape[dim], axis=dim)
        cells = jnp.concatenate(
            [
                lax.ppermute(tail, axis, [(i, (i + 1) % count) for i in range(count)]),
                cells,
                lax.ppermute(head, axis, [((i + 1) % count, i) for i in range(count)]),
            ],
            axis=dim,
        )
    return cells


def shift_component(positions_in, amount):
    marker = (jnp.arange(positions_in.shape[-2]) == 0).astype(jnp.float32)
    return positions_in + amount * marker[:, None]


def direction_rows(total, shares):
    order = np.arange(total, dtype=np.float64)
    height = 1.0 - (2.0 * order + 1.0) / total
    radius = np.sqrt(1.0 - height * height)
    turning = order * golden_turn
    share = total // shares
    table = np.zeros((shares, -(-share // 8) * 8, 128), np.float32)
    unit = np.stack([radius * np.cos(turning), radius * np.sin(turning), height], axis=1)
    table[:, :share, :3] = unit.reshape(shares, share, 3)
    return table


def directions_per_turn(share):
    return max(g for g in range(1, 6) if share % g == 0)


def store_powers(table, coords, half, cosines, sines):
    base = (
        table[:, 0:1] * coords[0:1] + table[:, 1:2] * coords[1:2] + table[:, 2:3] * coords[2:3]
    ) * (0.5 / half)
    count = table.shape[0]
    c1, s1 = jnp.cos(base), jnp.sin(base)
    powers = {1: (c1, s1)}
    for n in range(2, 9):
        (ca, sa), (cb, sb) = powers[n // 2], powers[n - n // 2]
        powers[n] = (ca * cb - sa * sb, sa * cb + ca * sb)
    for n in range(1, 9):
        for tile in range(base.shape[1] // 128):
            lanes = slice(tile * 128, (tile + 1) * 128)
            cosines[tile, (n - 1) * count : n * count, :] = powers[n][0][:, lanes]
            sines[tile, (n - 1) * count : n * count, :] = powers[n][1][:, lanes]


def rotated(features, direction, count, half, cosines, sines):
    rows = pl.ds(direction, 8, stride=count)
    last = pl.ds(7 * count + direction, 1)

    def across(held, at):
        return jnp.concatenate([held[tile, at, :] for tile in range(held.shape[0])], axis=1)

    cosine, sine = across(cosines, rows), across(sines, rows)
    step_c = jnp.broadcast_to(across(cosines, last), cosine.shape)
    step_s = jnp.broadcast_to(across(sines, last), sine.shape)
    double = 2.0 * step_c
    older = None
    low, high = [], []
    for first in range(0, half, 8):
        if first == 8:
            older = (cosine, sine)
            cosine, sine = cosine * step_c - sine * step_s, sine * step_c + cosine * step_s
        elif first > 8:
            held = (cosine, sine)
            cosine, sine = double * cosine - older[0], double * sine - older[1]
            older = held
        a = features[first : first + 8, :]
        b = features[half + first : half + first + 8, :]
        low.append(a * cosine - b * sine)
        high.append(b * cosine + a * sine)
    return [jnp.concatenate(low + high, axis=0).astype(jnp.bfloat16)]


def kv_kernel(chunk, share, live_ref, table_ref, coords_ref, rows_ref, weights_t_ref, weights_ref, states_ref, keys, cosines, sines):
    width = rows_ref.shape[1]
    half = width // 2
    count = table_ref.shape[0]
    per_turn = directions_per_turn(share)
    states_ref[...] = jnp.zeros_like(states_ref)
    live = live_ref[0]

    def advance(turn, carried):
        at = pl.ds(pl.multiple_of(turn * chunk, chunk), chunk)
        rows = rows_ref[at, :]
        keys[...] = lax.dot_general(
            weights_t_ref[width : 2 * width, :], rows, (((1,), (1,)), ((), ())),
            preferred_element_type=jnp.float32,
        )
        values = jnp.dot(rows, weights_ref[:, 2 * width :], preferred_element_type=jnp.float32)
        index = turn * chunk + lax.broadcasted_iota(jnp.int32, values.shape, 0)
        values = jnp.where(index < live, values, 0.0).astype(jnp.bfloat16)
        store_powers(table_ref[...], coords_ref[:, at], half, cosines, sines)

        def inner(group, held):
            parts = []
            for j in range(per_turn):
                parts += rotated(keys, group * per_turn + j, count, half, cosines, sines)
            size = per_turn * width
            out = pl.ds(pl.multiple_of(group * size, size), size)
            states_ref[out, :] += jnp.dot(
                jnp.concatenate(parts, axis=0), values, preferred_element_type=jnp.float32
            )
            return held

        return lax.fori_loop(0, share // per_turn, inner, carried)

    lax.fori_loop(0, (live + chunk - 1) // chunk, advance, 0)


def query_kernel(chunk, share, table_ref, coords_ref, rows_ref, weights_t_ref, states_ref, out_ref, queries, flipped, cosines, sines, total):
    atoms, width = rows_ref.shape
    half = width // 2
    count = table_ref.shape[0]
    per_turn = directions_per_turn(share)
    for d in range(share):
        flipped[:, d * width : (d + 1) * width] = states_ref[d * width : (d + 1) * width, :].T

    def advance(turn, carried):
        at = pl.ds(pl.multiple_of(turn * chunk, chunk), chunk)
        queries[...] = lax.dot_general(
            weights_t_ref[:width, :], rows_ref[at, :], (((1,), (1,)), ((), ())),
            preferred_element_type=jnp.float32,
        )
        store_powers(table_ref[...], coords_ref[:, at], half, cosines, sines)
        total[...] = jnp.zeros_like(total)

        def inner(group, held):
            parts = []
            for j in range(per_turn):
                parts += rotated(queries, group * per_turn + j, count, half, cosines, sines)
            size = per_turn * width
            columns = pl.ds(pl.multiple_of(group * size, size), size)
            total[...] += jnp.dot(
                flipped[:, columns], jnp.concatenate(parts, axis=0),
                preferred_element_type=jnp.float32,
            )
            return held

        lax.fori_loop(0, share // per_turn, inner, 0)
        out_ref[at, :] = total[...].T
        return carried

    lax.fori_loop(0, atoms // chunk, advance, 0)


def vmem(count):
    return [pl.BlockSpec(memory_space=pltpu.VMEM)] * count


def kv_states(live, table, coords, flat, weights_t, weights, share, padded_rows):
    width = flat.shape[1]
    chunk = 256
    count = table.shape[0]
    atoms = flat.shape[0] // 2
    return pl.pallas_call(
        functools.partial(kv_kernel, chunk, share),
        out_shape=jax.ShapeDtypeStruct((padded_rows, width), jnp.float32),
        in_specs=[pl.BlockSpec(memory_space=pltpu.SMEM)] + vmem(5),
        out_specs=pl.BlockSpec(memory_space=pltpu.VMEM),
        scratch_shapes=[
            pltpu.VMEM((width, chunk), jnp.float32),
            pltpu.VMEM((chunk // 128, 8 * count, 128), jnp.float32),
            pltpu.VMEM((chunk // 128, 8 * count, 128), jnp.float32),
        ],
        cost_estimate=pl.CostEstimate(
            flops=2 * share * atoms * width * width * 8, bytes_accessed=20_000_000, transcendentals=0
        ),
        name="kv_states",
    )(live, table, coords, flat, weights_t, weights)


def query_mix(table, coords, flat, weights_t, states, share):
    atoms, width = flat.shape
    chunk = 256
    count = table.shape[0]
    return pl.pallas_call(
        functools.partial(query_kernel, chunk, share),
        out_shape=jax.ShapeDtypeStruct((atoms, width), jnp.float32),
        in_specs=vmem(5),
        out_specs=pl.BlockSpec(memory_space=pltpu.VMEM),
        scratch_shapes=[
            pltpu.VMEM((width, chunk), jnp.float32),
            pltpu.VMEM((width, share * width), jnp.bfloat16),
            pltpu.VMEM((chunk // 128, 8 * count, 128), jnp.float32),
            pltpu.VMEM((chunk // 128, 8 * count, 128), jnp.float32),
            pltpu.VMEM((width, chunk), jnp.float32),
        ],
        cost_estimate=pl.CostEstimate(
            flops=2 * share * atoms * width * width * 8, bytes_accessed=20_000_000, transcendentals=0
        ),
        name="query_mix",
    )(table, coords, flat, weights_t, states)


def reduce_orders(bits):
    first = list(range(bits))
    second = list(first)
    if bits > 2:
        second[1], second[2] = second[2], second[1]
    return [first, second]


def reduce_kernel(bits, local_ref, out_ref, total, sent, landed, send_sems, recv_sems, gather_send, gather_recv):
    me = lax.axis_index("cell")

    def bit_of(b):
        return lax.rem(me // (1 << b), 2)

    def partner(b):
        return {"cell": me + (1 - 2 * bit_of(b)) * (1 << b)}

    barrier = pltpu.get_barrier_semaphore()
    for b in range(bits):
        pl.semaphore_signal(
            barrier, inc=1, device_id=partner(b), device_id_type=pl.DeviceIdType.MESH
        )
    orders = reduce_orders(bits)
    piece = local_ref.shape[0] // len(orders)
    starts = [k * piece for k in range(len(orders))]
    length = piece
    offset = 0
    for step in range(bits):
        half = length // 2
        copies = []
        for k, order in enumerate(orders):
            b = order[step]
            away = pl.multiple_of(starts[k] + (1 - bit_of(b)) * half, 16)
            at = pl.ds(k * piece + offset, half)
            source = local_ref if step == 0 else total
            sent[at, :] = source[pl.ds(away, half), :].astype(jnp.bfloat16)
            if step == 0 and k == 0:
                pl.semaphore_wait(barrier, bits)
            copy = pltpu.make_async_remote_copy(
                src_ref=sent.at[at, :],
                dst_ref=landed.at[at, :],
                send_sem=send_sems.at[k, step],
                recv_sem=recv_sems.at[k, step],
                device_id=partner(b),
                device_id_type=pl.DeviceIdType.MESH,
            )
            copy.start()
            copies.append(copy)
        for k, order in enumerate(orders):
            b = order[step]
            keep = pl.multiple_of(starts[k] + bit_of(b) * half, 16)
            at = pl.ds(k * piece + offset, half)
            source = local_ref if step == 0 else total
            copies[k].wait_recv()
            summed = source[pl.ds(keep, half), :] + landed[at, :].astype(jnp.float32)
            if step == bits - 1:
                out_ref[pl.ds(keep, half), :] = summed.astype(jnp.bfloat16)
            else:
                total[pl.ds(keep, half), :] = summed
            starts[k] = keep
        for copy in copies:
            copy.wait_send()
        length = half
        offset += half
    for step in reversed(range(bits)):
        copies = []
        for k, order in enumerate(orders):
            b = order[step]
            at = pl.ds(pl.multiple_of(starts[k], 16), length)
            copy = pltpu.make_async_remote_copy(
                src_ref=out_ref.at[at, :],
                dst_ref=out_ref.at[at, :],
                send_sem=gather_send.at[k, step],
                recv_sem=gather_recv.at[k, step],
                device_id=partner(b),
                device_id_type=pl.DeviceIdType.MESH,
            )
            copy.start()
            copies.append(copy)
        for k, order in enumerate(orders):
            copies[k].wait()
            starts[k] = starts[k] - bit_of(order[step]) * length
        length = 2 * length


def reduce_states(local, cells):
    bits = cells.bit_length() - 1
    rows, width = local.shape
    pieces = len(reduce_orders(bits))
    return pl.pallas_call(
        functools.partial(reduce_kernel, bits),
        out_shape=jax.ShapeDtypeStruct((rows, width), jnp.bfloat16),
        in_specs=vmem(1),
        out_specs=pl.BlockSpec(memory_space=pltpu.VMEM),
        scratch_shapes=[
            pltpu.VMEM((rows, width), jnp.float32),
            pltpu.VMEM((rows, width), jnp.bfloat16),
            pltpu.VMEM((rows, width), jnp.bfloat16),
        ]
        + [pltpu.SemaphoreType.DMA((pieces, bits))] * 4,
        compiler_params=pltpu.CompilerParams(collective_id=0, has_side_effects=True),
        name="reduce_states",
    )(local)


def radial_terms(own_positions, near_positions, near_features, filter_gains):
    differ = own_positions[:, None, :, :, None] - near_positions[:, :, :, None, :]
    distance = jnp.sqrt(jnp.sum(differ * differ, axis=2))
    centers = 2.0 + 2.0 * jnp.arange(filter_gains.shape[0], dtype=jnp.float32)
    scaled = (distance[:, :, None] - centers[None, None, :, None, None]) / radial_width
    radial = jnp.exp(-scaled * scaled).astype(jnp.bfloat16)
    summed = jnp.einsum(
        "gnkab,gnbf->gkaf", radial, near_features, preferred_element_type=jnp.float32
    )
    return jnp.sum(summed * filter_gains[None, :, None, :], axis=1)


def block_messages(
    first_slot,
    live_count,
    slot_count,
    group_width,
    neighbours,
    extended_features,
    extended_positions,
    filter_gains,
    face_blocks,
):
    initial = jnp.zeros(
        (slot_count, extended_features.shape[1], extended_features.shape[2]), jnp.float32
    )

    def block_advance(turn_index, running):
        start_slot = first_slot + turn_index * group_width
        picked = lax.dynamic_slice_in_dim(neighbours, start_slot, group_width, 0)
        near_features = extended_features[picked]
        near_positions = extended_positions[picked]
        own_positions = lax.dynamic_slice_in_dim(
            extended_positions, start_slot + face_blocks, group_width, 0
        )
        result = radial_terms(own_positions, near_positions, near_features, filter_gains)
        return lax.dynamic_update_slice_in_dim(running, result, turn_index * group_width, 0)

    group_total = (live_count + group_width - 1) // group_width
    return lax.fori_loop(0, group_total, block_advance, initial)


def per_device(
    atom_features, positions, neighbours, counts, filter_gains, w_update, projections, w_output
):
    cells = lax.axis_size("cell")
    cell_index = lax.axis_index("cell")
    dirs_count = lax.axis_size("dir")
    dir_index = lax.axis_index("dir")
    capacity, block_atoms, width = atom_features.shape
    balanced_blocks = capacity // 2
    face_blocks = H
    faces_features, faces_positions = (
        extended(atom_features[:face_blocks], (("cell", 0),), face_blocks),
        extended(positions[:face_blocks], (("cell", 0),), face_blocks),
    )
    float_positions = positions.astype(jnp.float32)
    faces_float = faces_positions.astype(jnp.float32)
    extended_features = jnp.concatenate(
        [faces_features[:face_blocks], atom_features, faces_features[2 * face_blocks :]], axis=0
    )
    extended_positions = jnp.concatenate(
        [
            shift_component(faces_float[:face_blocks], -slab_width),
            float_positions,
            shift_component(faces_float[2 * face_blocks :], slab_width),
        ],
        axis=0,
    )
    own_count = counts[cell_index]
    share_slots = capacity // dirs_count
    first_slot = dir_index * share_slots
    live_count = jnp.clip(own_count - first_slot, 0, share_slots)
    message = block_messages(
        first_slot,
        live_count,
        share_slots,
        2,
        neighbours,
        extended_features,
        extended_positions,
        filter_gains,
        face_blocks,
    )
    own_features = lax.dynamic_slice_in_dim(atom_features, first_slot, share_slots, 0)
    activated = jax.nn.silu(message).astype(jnp.bfloat16)
    updated_share = (
        own_features.astype(jnp.float32)
        + jnp.dot(activated, w_update, preferred_element_type=jnp.float32)
    ).astype(jnp.bfloat16)
    updated = lax.all_gather(updated_share, "dir", axis=0, tiled=True)
    count_ends = jnp.cumsum(counts)
    starts = count_ends - counts
    first_live = starts[cell_index]
    slot_cap = max(1, 2 * balanced_blocks // cells)
    period = cells * slot_cap
    slot_order = jnp.arange(period, dtype=jnp.int32)
    offset = (slot_order - first_live) % period
    is_live = offset < own_count
    rows_picked = jnp.where(is_live, offset, 0)
    send_features = jnp.where(
        is_live[:, None, None], updated[rows_picked], jnp.zeros((), jnp.bfloat16)
    )
    send_positions = jnp.where(
        is_live[:, None, None], positions[rows_picked], jnp.zeros((), jnp.bfloat16)
    )
    received_features, received_positions = (
        lax.all_to_all(send_features, "cell", split_axis=0, concat_axis=0, tiled=True),
        lax.all_to_all(send_positions, "cell", split_axis=0, concat_axis=0, tiled=True),
    )
    target = jnp.arange(balanced_blocks, dtype=jnp.int32)
    within = target % slot_cap
    global_index = (target // slot_cap * cells + cell_index) * slot_cap + within
    source = jnp.sum((count_ends[None, :] <= global_index[:, None]).astype(jnp.int32), axis=1)
    pick_rows = source * slot_cap + within
    balanced_features = received_features[pick_rows]
    balanced_positions = shift_component(
        received_positions[pick_rows].astype(jnp.float32),
        slab_width * source.astype(jnp.float32)[:, None, None],
    )
    share = DIRS // dirs_count
    unit_rows = 32 * cells
    padded_rows = -(-share * width // unit_rows) * unit_rows
    table = lax.dynamic_index_in_dim(
        jnp.asarray(direction_rows(DIRS, dirs_count)), dir_index, 0, keepdims=False
    )
    weights_t = projections.T
    own_global = shift_component(float_positions, slab_width * cell_index.astype(jnp.float32))
    own_coords = jnp.transpose(own_global, (1, 0, 2)).reshape(3, -1)
    live_atoms = (own_count * block_atoms).astype(jnp.int32).reshape(1)
    local_states = kv_states(
        live_atoms, table, own_coords, updated.reshape(-1, width), weights_t, projections, share, padded_rows
    )
    states = reduce_states(local_states, cells)
    share_blocks = balanced_blocks // dirs_count

    def partial_mix(owner):
        features = lax.dynamic_slice_in_dim(balanced_features, owner * share_blocks, share_blocks, 0)
        places = lax.dynamic_slice_in_dim(balanced_positions, owner * share_blocks, share_blocks, 0)
        coords = jnp.transpose(places, (1, 0, 2)).reshape(3, -1)
        return query_mix(table, coords, features.reshape(-1, width), weights_t, states, share)

    mixed_rows = None
    for hop in range(1, dirs_count):
        away = partial_mix((dir_index + hop) % dirs_count).astype(jnp.bfloat16)
        came = lax.ppermute(away, "dir", [(i, (i + hop) % dirs_count) for i in range(dirs_count)])
        came = came.astype(jnp.float32)
        mixed_rows = came if mixed_rows is None else mixed_rows + came
    kept = partial_mix(dir_index)
    mixed_rows = kept if mixed_rows is None else kept + mixed_rows
    mix_scale = 1.0 / math.sqrt(DIRS * cells * balanced_blocks * block_atoms * width)
    mixed = (mixed_rows * mix_scale).astype(jnp.bfloat16)
    attended = jnp.dot(mixed, w_output, preferred_element_type=jnp.float32).astype(jnp.bfloat16)
    return attended.reshape(-1, block_atoms, width)


def solution(mesh):
    placed = (
        P("cell", None, None),
        P("cell", None, None),
        P("cell", None),
        P(),
        P(),
        P(),
        P(),
        P(),
    )
    return jax.shard_map(
        per_device,
        mesh=mesh,
        in_specs=placed,
        out_specs=P(("cell", "dir"), None, None),
        check_vma=False,
    )
```

```python
import functools
import math

import jax
import jax.numpy as jnp
import numpy as np
from jax import lax
from jax.experimental import pallas as pl
from jax.experimental.pallas import tpu as pltpu
from jax.sharding import PartitionSpec as P

DIRS = 50
H = 4


slab_width = 12.0
radial_width = 0.6
golden_turn = math.pi * (3.0 - math.sqrt(5.0))


def shift_component(positions_in, amount):
    marker = (jnp.arange(positions_in.shape[-2]) == 0).astype(jnp.float32)
    return positions_in + amount * marker[:, None]


def direction_rows(total, shares):
    order = np.arange(total, dtype=np.float64)
    height = 1.0 - (2.0 * order + 1.0) / total
    radius = np.sqrt(1.0 - height * height)
    turning = order * golden_turn
    share = total // shares
    table = np.zeros((shares, -(-share // 8) * 8, 128), np.float32)
    unit = np.stack([radius * np.cos(turning), radius * np.sin(turning), height], axis=1)
    table[:, :share, :3] = unit.reshape(shares, share, 3)
    return table


def directions_per_turn(share):
    return max(g for g in range(1, 6) if share % g == 0)


def store_powers(table, coords, half, cosines, sines):
    base = (
        table[:, 0:1] * coords[0:1] + table[:, 1:2] * coords[1:2] + table[:, 2:3] * coords[2:3]
    ) * (0.5 / half)
    count = table.shape[0]
    c1, s1 = jnp.cos(base), jnp.sin(base)
    powers = {1: (c1, s1)}
    for n in range(2, 9):
        (ca, sa), (cb, sb) = powers[n // 2], powers[n - n // 2]
        powers[n] = (ca * cb - sa * sb, sa * cb + ca * sb)
    for n in range(1, 9):
        for tile in range(base.shape[1] // 128):
            lanes = slice(tile * 128, (tile + 1) * 128)
            cosines[tile, (n - 1) * count : n * count, :] = powers[n][0][:, lanes]
            sines[tile, (n - 1) * count : n * count, :] = powers[n][1][:, lanes]


def rotated(features, direction, count, half, cosines, sines):
    rows = pl.ds(direction, 8, stride=count)
    last = pl.ds(7 * count + direction, 1)

    def across(held, at):
        return jnp.concatenate([held[tile, at, :] for tile in range(held.shape[0])], axis=1)

    cosine, sine = across(cosines, rows), across(sines, rows)
    step_c = jnp.broadcast_to(across(cosines, last), cosine.shape)
    step_s = jnp.broadcast_to(across(sines, last), sine.shape)
    double = 2.0 * step_c
    older = None
    low, high = [], []
    for first in range(0, half, 8):
        if first == 8:
            older = (cosine, sine)
            cosine, sine = cosine * step_c - sine * step_s, sine * step_c + cosine * step_s
        elif first > 8:
            held = (cosine, sine)
            cosine, sine = double * cosine - older[0], double * sine - older[1]
            older = held
        a = features[first : first + 8, :]
        b = features[half + first : half + first + 8, :]
        low.append(a * cosine - b * sine)
        high.append(b * cosine + a * sine)
    return [jnp.concatenate(low + high, axis=0).astype(jnp.bfloat16)]


def kv_kernel(chunk, share, live_ref, table_ref, coords_ref, rows_ref, weights_t_ref, weights_ref, out_ref, states_ref, keys, cosines, sines):
    width = rows_ref.shape[1]
    half = width // 2
    count = table_ref.shape[0]
    per_turn = directions_per_turn(share)
    states_ref[...] = jnp.zeros_like(states_ref)
    live = live_ref[0]

    def advance(turn, carried):
        at = pl.ds(pl.multiple_of(turn * chunk, chunk), chunk)
        rows = rows_ref[at, :]
        keys[...] = lax.dot_general(
            weights_t_ref[width : 2 * width, :], rows, (((1,), (1,)), ((), ())),
            preferred_element_type=jnp.float32,
        )
        values = jnp.dot(rows, weights_ref[:, 2 * width :], preferred_element_type=jnp.float32)
        index = turn * chunk + lax.broadcasted_iota(jnp.int32, values.shape, 0)
        values = jnp.where(index < live, values, 0.0).astype(jnp.bfloat16)
        store_powers(table_ref[...], coords_ref[:, at], half, cosines, sines)

        def inner(group, held):
            parts = []
            for j in range(per_turn):
                parts += rotated(keys, group * per_turn + j, count, half, cosines, sines)
            size = per_turn * width
            out = pl.ds(pl.multiple_of(group * size, size), size)
            states_ref[out, :] += jnp.dot(
                jnp.concatenate(parts, axis=0), values, preferred_element_type=jnp.float32
            )
            return held

        return lax.fori_loop(0, share // per_turn, inner, carried)

    lax.fori_loop(0, (live + chunk - 1) // chunk, advance, 0)
    out_ref[...] = states_ref[...].astype(out_ref.dtype)


def query_kernel(chunk, share, table_ref, coords_ref, rows_ref, weights_t_ref, states_ref, out_ref, queries, flipped, cosines, sines, total):
    atoms, width = rows_ref.shape
    half = width // 2
    count = table_ref.shape[0]
    per_turn = directions_per_turn(share)
    for d in range(share):
        flipped[:, d * width : (d + 1) * width] = states_ref[d * width : (d + 1) * width, :].T

    def advance(turn, carried):
        at = pl.ds(pl.multiple_of(turn * chunk, chunk), chunk)
        queries[...] = lax.dot_general(
            weights_t_ref[:width, :], rows_ref[at, :], (((1,), (1,)), ((), ())),
            preferred_element_type=jnp.float32,
        )
        store_powers(table_ref[...], coords_ref[:, at], half, cosines, sines)
        total[...] = jnp.zeros_like(total)

        def inner(group, held):
            parts = []
            for j in range(per_turn):
                parts += rotated(queries, group * per_turn + j, count, half, cosines, sines)
            size = per_turn * width
            columns = pl.ds(pl.multiple_of(group * size, size), size)
            total[...] += jnp.dot(
                flipped[:, columns], jnp.concatenate(parts, axis=0),
                preferred_element_type=jnp.float32,
            )
            return held

        lax.fori_loop(0, share // per_turn, inner, 0)
        out_ref[at, :] = total[...].T
        return carried

    lax.fori_loop(0, atoms // chunk, advance, 0)


def vmem(count):
    return [pl.BlockSpec(memory_space=pltpu.VMEM)] * count


def kv_states(live, table, coords, flat, weights_t, weights, share, padded_rows, dtype):
    width = flat.shape[1]
    chunk = 256
    count = table.shape[0]
    atoms = flat.shape[0] // 2
    return pl.pallas_call(
        functools.partial(kv_kernel, chunk, share),
        out_shape=jax.ShapeDtypeStruct((padded_rows, width), dtype),
        in_specs=[pl.BlockSpec(memory_space=pltpu.SMEM)] + vmem(5),
        out_specs=pl.BlockSpec(memory_space=pltpu.VMEM),
        scratch_shapes=[
            pltpu.VMEM((padded_rows, width), jnp.float32),
            pltpu.VMEM((width, chunk), jnp.float32),
            pltpu.VMEM((chunk // 128, 8 * count, 128), jnp.float32),
            pltpu.VMEM((chunk // 128, 8 * count, 128), jnp.float32),
        ],
        cost_estimate=pl.CostEstimate(
            flops=2 * share * atoms * width * width * 8, bytes_accessed=20_000_000, transcendentals=0
        ),
        name="kv_states",
    )(live, table, coords, flat, weights_t, weights)


def query_mix(table, coords, flat, weights_t, states, share):
    atoms, width = flat.shape
    chunk = 256
    count = table.shape[0]
    return pl.pallas_call(
        functools.partial(query_kernel, chunk, share),
        out_shape=jax.ShapeDtypeStruct((atoms, width), jnp.float32),
        in_specs=vmem(5),
        out_specs=pl.BlockSpec(memory_space=pltpu.VMEM),
        scratch_shapes=[
            pltpu.VMEM((width, chunk), jnp.float32),
            pltpu.VMEM((width, share * width), jnp.bfloat16),
            pltpu.VMEM((chunk // 128, 8 * count, 128), jnp.float32),
            pltpu.VMEM((chunk // 128, 8 * count, 128), jnp.float32),
            pltpu.VMEM((width, chunk), jnp.float32),
        ],
        cost_estimate=pl.CostEstimate(
            flops=2 * share * atoms * width * width * 8, bytes_accessed=20_000_000, transcendentals=0
        ),
        name="query_mix",
    )(table, coords, flat, weights_t, states)


def reduce_orders(bits):
    first = list(range(bits))
    second = list(first)
    if bits > 2:
        second[1], second[2] = second[2], second[1]
    return [first, second]


def piece_rows(rows, unit, pieces):
    units = rows // unit
    return [(units // pieces + (k < units % pieces)) * unit for k in range(pieces)]


def reduce_kernel(bits, local_ref, came_ref, out_ref, total, sent, landed, send_sems, recv_sems, gather_send, gather_recv):
    me = lax.axis_index("cell")

    def bit_of(b):
        return lax.rem(me // (1 << b), 2)

    def partner(b):
        return {"cell": me + (1 - 2 * bit_of(b)) * (1 << b)}

    barrier = pltpu.get_barrier_semaphore()
    for b in range(bits):
        pl.semaphore_signal(
            barrier, inc=1, device_id=partner(b), device_id_type=pl.DeviceIdType.MESH
        )
    orders = reduce_orders(bits)
    lengths = piece_rows(local_ref.shape[0], 16 * (1 << bits), len(orders))
    starts = [sum(lengths[:k]) for k in range(len(orders))]
    offsets = list(starts)

    def own(step, at):
        if step == 0:
            return local_ref[at, :] + came_ref[at, :].astype(jnp.float32)
        return total[at, :]

    for step in range(bits):
        copies = []
        for k, order in enumerate(orders):
            b, half = order[step], lengths[k] // 2
            away = pl.multiple_of(starts[k] + (1 - bit_of(b)) * half, 16)
            at = pl.ds(offsets[k], half)
            sent[at, :] = own(step, pl.ds(away, half)).astype(jnp.bfloat16)
            if step == 0 and k == 0:
                pl.semaphore_wait(barrier, bits)
            copy = pltpu.make_async_remote_copy(
                src_ref=sent.at[at, :],
                dst_ref=landed.at[at, :],
                send_sem=send_sems.at[k, step],
                recv_sem=recv_sems.at[k, step],
                device_id=partner(b),
                device_id_type=pl.DeviceIdType.MESH,
            )
            copy.start()
            copies.append(copy)
        for k, order in enumerate(orders):
            b, half = order[step], lengths[k] // 2
            keep = pl.multiple_of(starts[k] + bit_of(b) * half, 16)
            at = pl.ds(offsets[k], half)
            copies[k].wait_recv()
            summed = own(step, pl.ds(keep, half)) + landed[at, :].astype(jnp.float32)
            if step == bits - 1:
                out_ref[pl.ds(keep, half), :] = summed.astype(jnp.bfloat16)
            else:
                total[pl.ds(keep, half), :] = summed
            starts[k] = keep
            lengths[k] = half
            offsets[k] += half
        for copy in copies:
            copy.wait_send()
    for step in reversed(range(bits)):
        copies = []
        for k, order in enumerate(orders):
            at = pl.ds(pl.multiple_of(starts[k], 16), lengths[k])
            copy = pltpu.make_async_remote_copy(
                src_ref=out_ref.at[at, :],
                dst_ref=out_ref.at[at, :],
                send_sem=gather_send.at[k, step],
                recv_sem=gather_recv.at[k, step],
                device_id=partner(order[step]),
                device_id_type=pl.DeviceIdType.MESH,
            )
            copy.start()
            copies.append(copy)
        for k, order in enumerate(orders):
            copies[k].wait()
            starts[k] = starts[k] - bit_of(order[step]) * lengths[k]
            lengths[k] = 2 * lengths[k]


def reduce_states(local, came, cells):
    bits = cells.bit_length() - 1
    rows, width = local.shape
    pieces = len(reduce_orders(bits))
    return pl.pallas_call(
        functools.partial(reduce_kernel, bits),
        out_shape=jax.ShapeDtypeStruct((rows, width), jnp.bfloat16),
        in_specs=vmem(2),
        out_specs=pl.BlockSpec(memory_space=pltpu.VMEM),
        scratch_shapes=[
            pltpu.VMEM((rows, width), jnp.float32),
            pltpu.VMEM((rows, width), jnp.bfloat16),
            pltpu.VMEM((rows, width), jnp.bfloat16),
        ]
        + [pltpu.SemaphoreType.DMA((pieces, bits))] * 4,
        compiler_params=pltpu.CompilerParams(collective_id=0, has_side_effects=True),
        cost_estimate=pl.CostEstimate(flops=20_000_000_000, bytes_accessed=60_000_000, transcendentals=0),
        name="reduce_states",
    )(local, came)


def radial_terms(own_positions, near_positions, near_features, filter_gains):
    differ = own_positions[:, None, :, :, None] - near_positions[:, :, :, None, :]
    distance = jnp.sqrt(jnp.sum(differ * differ, axis=2))
    centers = 2.0 + 2.0 * jnp.arange(filter_gains.shape[0], dtype=jnp.float32)
    scaled = (distance[:, :, None] - centers[None, None, :, None, None]) / radial_width
    radial = jnp.exp(-scaled * scaled).astype(jnp.bfloat16)
    summed = jnp.einsum(
        "gnkab,gnbf->gkaf", radial, near_features, preferred_element_type=jnp.float32
    )
    return jnp.sum(summed * filter_gains[None, :, None, :], axis=1)


def block_messages(live_count, group_width, picks, own_positions, extended_features, extended_positions, filter_gains):
    slot_count = picks.shape[0]
    initial = jnp.zeros(
        (slot_count, extended_features.shape[1], extended_features.shape[2]), jnp.float32
    )

    def block_advance(turn_index, running):
        at = turn_index * group_width
        picked = lax.dynamic_slice_in_dim(picks, at, group_width, 0)
        near_features = extended_features[picked]
        near_positions = extended_positions[picked]
        own = lax.dynamic_slice_in_dim(own_positions, at, group_width, 0)
        result = radial_terms(own, near_positions, near_features, filter_gains)
        return lax.dynamic_update_slice_in_dim(running, result, at, 0)

    group_total = (live_count + group_width - 1) // group_width
    return lax.fori_loop(0, group_total, block_advance, initial)


def join(features, places):
    padded = jnp.pad(places, ((0, 0), (0, 16 - places.shape[1]), (0, 0)))
    return jnp.concatenate([features, padded], axis=1)


def per_device(
    atom_features, positions, neighbours, counts, filter_gains, w_update, projections, w_output
):
    cells = lax.axis_size("cell")
    cell_index = lax.axis_index("cell")
    dirs_count = lax.axis_size("dir")
    dir_index = lax.axis_index("dir")
    capacity, block_atoms, width = atom_features.shape
    balanced_blocks = capacity // 2
    face_blocks = H
    faces = join(atom_features[:face_blocks], positions[:face_blocks])
    before = lax.ppermute(faces, "cell", [(i, (i + 1) % cells) for i in range(cells)])
    after = lax.ppermute(faces, "cell", [((i + 1) % cells, i) for i in range(cells)])
    float_positions = positions.astype(jnp.float32)
    extended_features = jnp.concatenate(
        [before[:, :block_atoms], atom_features, after[:, :block_atoms]], axis=0
    )
    axes = positions.shape[1]
    places_of = slice(block_atoms, block_atoms + axes)
    extended_positions = jnp.concatenate(
        [
            shift_component(before[:, places_of].astype(jnp.float32), -slab_width),
            float_positions,
            shift_component(after[:, places_of].astype(jnp.float32), slab_width),
        ],
        axis=0,
    )
    own_count = counts[cell_index]
    count_ends = jnp.cumsum(counts)
    first_live = (count_ends - counts)[cell_index]
    share_slots = capacity // dirs_count
    first_slot = (dir_index - first_live) % dirs_count

    def mine(array):
        dealt = array.reshape((share_slots, dirs_count) + array.shape[1:])
        return lax.dynamic_index_in_dim(dealt, first_slot, 1, keepdims=False)

    live_count = (own_count - first_slot + dirs_count - 1) // dirs_count
    own_features = mine(atom_features)
    own_places = mine(positions)
    own_float = own_places.astype(jnp.float32)
    message = block_messages(
        live_count, 2, mine(neighbours), own_float, extended_features, extended_positions, filter_gains
    )
    activated = jax.nn.silu(message).astype(jnp.bfloat16)
    updated = (
        own_features.astype(jnp.float32)
        + jnp.dot(activated, w_update, preferred_element_type=jnp.float32)
    ).astype(jnp.bfloat16)

    share = DIRS // dirs_count
    unit_rows = 16 * cells
    padded_rows = -(-share * width // unit_rows) * unit_rows
    tables = jnp.asarray(direction_rows(DIRS, dirs_count))
    weights_t = projections.T
    own_global = shift_component(own_float, slab_width * cell_index.astype(jnp.float32))
    own_coords = jnp.transpose(own_global, (1, 0, 2)).reshape(axes, -1)
    live_atoms = (live_count * block_atoms).astype(jnp.int32).reshape(1)

    def states_of(owner, dtype):
        part = lax.dynamic_index_in_dim(tables, owner, 0, keepdims=False)
        return kv_states(
            live_atoms, part, own_coords, updated.reshape(-1, width), weights_t, projections, share,
            padded_rows, dtype,
        )

    came = jnp.zeros((padded_rows, width), jnp.bfloat16)
    for hop in range(1, dirs_count):
        away = states_of((dir_index + hop) % dirs_count, jnp.bfloat16)
        arrived = lax.ppermute(away, "dir", [(i, (i + hop) % dirs_count) for i in range(dirs_count)])
        came = arrived if hop == 1 else came + arrived
    local_states = states_of(dir_index, jnp.float32)
    states = reduce_states(local_states, came, cells)

    slot_cap = max(1, 2 * balanced_blocks // cells)
    period = cells * slot_cap
    owner = jnp.arange(cells, dtype=jnp.int32)
    whole_rounds = slot_cap % dirs_count == 0
    per_owner = slot_cap // dirs_count if whole_rounds else slot_cap
    lane = jnp.arange(per_owner, dtype=jnp.int32)
    if whole_rounds:
        wanted = owner[:, None] * slot_cap + lane[None, :] * dirs_count + dir_index
    else:
        wanted = owner[:, None] * slot_cap + lane[None, :]
    offset = ((wanted - first_live) % period).reshape(-1)
    index = (offset - first_slot) // dirs_count
    is_mine = (offset < own_count) & ((offset - first_slot) % dirs_count == 0)
    picked = jnp.where(is_mine, index, 0)
    parcels = jnp.where(
        is_mine[:, None, None], join(updated, own_places)[picked], jnp.zeros((), jnp.bfloat16)
    )
    received = lax.all_to_all(parcels, "cell", split_axis=0, concat_axis=0, tiled=True)
    target = jnp.arange(balanced_blocks, dtype=jnp.int32)
    global_index = (target // slot_cap * cells + cell_index) * slot_cap + target % slot_cap
    source = jnp.sum((count_ends[None, :] <= global_index[:, None]).astype(jnp.int32), axis=1)
    if whole_rounds:
        def dealt_to(array, part):
            split = array.reshape((-1, dirs_count) + array.shape[1:])
            return lax.dynamic_index_in_dim(split, part, 1, keepdims=False)

        within = dealt_to(target % slot_cap, dir_index) // dirs_count
        rows = received[dealt_to(source, dir_index) * per_owner + within]
        gathered = [rows]
        for hop in range(1, dirs_count):
            gathered.append(
                lax.ppermute(rows, "dir", [(i, (i + hop) % dirs_count) for i in range(dirs_count)])
            )
        parts = jnp.stack(gathered, axis=1)
        order = (dir_index - jnp.arange(dirs_count, dtype=jnp.int32)) % dirs_count
        balanced = parts[:, order].reshape((balanced_blocks,) + parts.shape[2:])
    else:
        rows = received[source * per_owner + target % slot_cap]
        balanced = rows
        for hop in range(1, dirs_count):
            other = lax.ppermute(rows, "dir", [(i, (i + hop) % dirs_count) for i in range(dirs_count)])
            held = global_index % dirs_count == (dir_index - hop) % dirs_count
            balanced = jnp.where(held[:, None, None], other, balanced)
    balanced_features = balanced[:, :block_atoms]
    balanced_positions = shift_component(
        balanced[:, places_of].astype(jnp.float32),
        slab_width * source.astype(jnp.float32)[:, None, None],
    )
    share_blocks = balanced_blocks // dirs_count
    table = lax.dynamic_index_in_dim(tables, dir_index, 0, keepdims=False)

    def partial_mix(owner):
        features = lax.dynamic_slice_in_dim(balanced_features, owner * share_blocks, share_blocks, 0)
        places = lax.dynamic_slice_in_dim(balanced_positions, owner * share_blocks, share_blocks, 0)
        coords = jnp.transpose(places, (1, 0, 2)).reshape(axes, -1)
        return query_mix(table, coords, features.reshape(-1, width), weights_t, states, share)

    mixed_rows = None
    for hop in range(1, dirs_count):
        away = partial_mix((dir_index + hop) % dirs_count).astype(jnp.bfloat16)
        arrived = lax.ppermute(away, "dir", [(i, (i + hop) % dirs_count) for i in range(dirs_count)])
        arrived = arrived.astype(jnp.float32)
        mixed_rows = arrived if mixed_rows is None else mixed_rows + arrived
    kept = partial_mix(dir_index)
    mixed_rows = kept if mixed_rows is None else kept + mixed_rows
    mix_scale = 1.0 / math.sqrt(DIRS * cells * balanced_blocks * block_atoms * width)
    mixed = (mixed_rows * mix_scale).astype(jnp.bfloat16)
    attended = jnp.dot(mixed, w_output, preferred_element_type=jnp.float32).astype(jnp.bfloat16)
    return attended.reshape(-1, block_atoms, width)


def solution(mesh):
    placed = (
        P("cell", None, None),
        P("cell", None, None),
        P("cell", None),
        P(),
        P(),
        P(),
        P(),
        P(),
    )
    return jax.shard_map(
        per_device,
        mesh=mesh,
        in_specs=placed,
        out_specs=P(("cell", "dir"), None, None),
        check_vma=False,
    )
```

```python
import functools
import math

import jax
import jax.numpy as jnp
import numpy as np
from jax import lax
from jax.experimental import pallas as pl
from jax.experimental.pallas import tpu as pltpu
from jax.sharding import PartitionSpec as P

DIRS = 50
H = 4


slab_width = 12.0
radial_width = 0.6
golden_turn = math.pi * (3.0 - math.sqrt(5.0))


def shift_component(positions_in, amount):
    marker = (jnp.arange(positions_in.shape[-2]) == 0).astype(jnp.float32)
    return positions_in + amount * marker[:, None]


def direction_rows(total, shares):
    order = np.arange(total, dtype=np.float64)
    height = 1.0 - (2.0 * order + 1.0) / total
    radius = np.sqrt(1.0 - height * height)
    turning = order * golden_turn
    share = total // shares
    table = np.zeros((shares, -(-share // 8) * 8, 128), np.float32)
    unit = np.stack([radius * np.cos(turning), radius * np.sin(turning), height], axis=1)
    table[:, :share, :3] = unit.reshape(shares, share, 3)
    return table


def directions_per_turn(share):
    return max(g for g in range(1, 6) if share % g == 0)


def store_powers(table, coords, half, cosines, sines):
    base = (
        table[:, 0:1] * coords[0:1] + table[:, 1:2] * coords[1:2] + table[:, 2:3] * coords[2:3]
    ) * (0.5 / half)
    count = table.shape[0]
    c1, s1 = jnp.cos(base), jnp.sin(base)
    powers = {1: (c1, s1)}
    for n in range(2, 9):
        (ca, sa), (cb, sb) = powers[n // 2], powers[n - n // 2]
        powers[n] = (ca * cb - sa * sb, sa * cb + ca * sb)
    for n in range(1, 9):
        for tile in range(base.shape[1] // 128):
            lanes = slice(tile * 128, (tile + 1) * 128)
            cosines[tile, (n - 1) * count : n * count, :] = powers[n][0][:, lanes]
            sines[tile, (n - 1) * count : n * count, :] = powers[n][1][:, lanes]


def rotated(features, direction, count, half, cosines, sines):
    rows = pl.ds(direction, 8, stride=count)
    last = pl.ds(7 * count + direction, 1)

    def across(held, at):
        return jnp.concatenate([held[tile, at, :] for tile in range(held.shape[0])], axis=1)

    cosine, sine = across(cosines, rows), across(sines, rows)
    step_c = jnp.broadcast_to(across(cosines, last), cosine.shape)
    step_s = jnp.broadcast_to(across(sines, last), sine.shape)
    double = 2.0 * step_c
    older = None
    turned = []
    for first in range(0, half, 8):
        if first == 8:
            older = (cosine, sine)
            cosine, sine = cosine * step_c - sine * step_s, sine * step_c + cosine * step_s
        elif first > 8:
            held = (cosine, sine)
            cosine, sine = double * cosine - older[0], double * sine - older[1]
            older = held
        turned.append((cosine, sine))
    low, high = [], []
    for first in range(0, half, 16):
        pair = turned[first // 8 : first // 8 + 2]
        cosine, sine = [
            jnp.concatenate([both[which] for both in pair], axis=0).astype(jnp.bfloat16)
            for which in range(2)
        ]
        a = features[first : first + 16, :]
        b = features[half + first : half + first + 16, :]
        low.append(a * cosine - b * sine)
        high.append(b * cosine + a * sine)
    return [jnp.concatenate(low + high, axis=0)]


def kv_kernel(chunk, share, live_ref, table_ref, coords_ref, rows_ref, weights_t_ref, weights_ref, out_ref, states_ref, keys, cosines, sines):
    width = rows_ref.shape[1]
    half = width // 2
    count = table_ref.shape[0]
    per_turn = directions_per_turn(share)
    states_ref[...] = jnp.zeros_like(states_ref)
    live = live_ref[0]

    def advance(turn, carried):
        at = pl.ds(pl.multiple_of(turn * chunk, chunk), chunk)
        rows = rows_ref[at, :]
        keys[...] = lax.dot_general(
            weights_t_ref[width : 2 * width, :], rows, (((1,), (1,)), ((), ())),
            preferred_element_type=jnp.float32,
        ).astype(jnp.bfloat16)
        values = jnp.dot(rows, weights_ref[:, 2 * width :], preferred_element_type=jnp.float32)
        index = turn * chunk + lax.broadcasted_iota(jnp.int32, values.shape, 0)
        values = jnp.where(index < live, values, 0.0).astype(jnp.bfloat16)
        store_powers(table_ref[...], coords_ref[:, at], half, cosines, sines)

        for group in range(share // per_turn):
            parts = []
            for j in range(per_turn):
                parts += rotated(keys, group * per_turn + j, count, half, cosines, sines)
            size = per_turn * width
            states_ref[group * size : (group + 1) * size, :] += jnp.dot(
                jnp.concatenate(parts, axis=0), values, preferred_element_type=jnp.float32
            )
        return carried

    lax.fori_loop(0, (live + chunk - 1) // chunk, advance, 0)
    out_ref[...] = states_ref[...].astype(out_ref.dtype)


def query_kernel(chunk, share, table_ref, coords_ref, rows_ref, weights_t_ref, states_ref, out_ref, queries, flipped, cosines, sines):
    atoms, width = rows_ref.shape
    half = width // 2
    count = table_ref.shape[0]
    per_turn = directions_per_turn(share)
    for d in range(share):
        flipped[:, d * width : (d + 1) * width] = states_ref[d * width : (d + 1) * width, :].T

    def advance(turn, carried):
        at = pl.ds(pl.multiple_of(turn * chunk, chunk), chunk)
        queries[...] = lax.dot_general(
            weights_t_ref[:width, :], rows_ref[at, :], (((1,), (1,)), ((), ())),
            preferred_element_type=jnp.float32,
        ).astype(jnp.bfloat16)
        store_powers(table_ref[...], coords_ref[:, at], half, cosines, sines)
        summed = None
        for group in range(share // per_turn):
            parts = []
            for j in range(per_turn):
                parts += rotated(queries, group * per_turn + j, count, half, cosines, sines)
            size = per_turn * width
            term = jnp.dot(
                flipped[:, group * size : (group + 1) * size], jnp.concatenate(parts, axis=0),
                preferred_element_type=jnp.float32,
            )
            summed = term if summed is None else summed + term
        out_ref[at, :] = summed.T
        return carried

    lax.fori_loop(0, atoms // chunk, advance, 0)


def vmem(count):
    return [pl.BlockSpec(memory_space=pltpu.VMEM)] * count


def kv_states(live, table, coords, flat, weights_t, weights, share, padded_rows, dtype):
    width = flat.shape[1]
    chunk = 256
    count = table.shape[0]
    atoms = flat.shape[0] // 2
    return pl.pallas_call(
        functools.partial(kv_kernel, chunk, share),
        out_shape=jax.ShapeDtypeStruct((padded_rows, width), dtype),
        in_specs=[pl.BlockSpec(memory_space=pltpu.SMEM)] + vmem(5),
        out_specs=pl.BlockSpec(memory_space=pltpu.VMEM),
        scratch_shapes=[
            pltpu.VMEM((padded_rows, width), jnp.float32),
            pltpu.VMEM((width, chunk), jnp.bfloat16),
            pltpu.VMEM((chunk // 128, 8 * count, 128), jnp.float32),
            pltpu.VMEM((chunk // 128, 8 * count, 128), jnp.float32),
        ],
        cost_estimate=pl.CostEstimate(
            flops=2 * share * atoms * width * width * 8, bytes_accessed=20_000_000, transcendentals=0
        ),
        name="kv_states",
    )(live, table, coords, flat, weights_t, weights)


def query_mix(table, coords, flat, weights_t, states, share):
    atoms, width = flat.shape
    chunk = 256
    count = table.shape[0]
    return pl.pallas_call(
        functools.partial(query_kernel, chunk, share),
        out_shape=jax.ShapeDtypeStruct((atoms, width), jnp.float32),
        in_specs=vmem(5),
        out_specs=pl.BlockSpec(memory_space=pltpu.VMEM),
        scratch_shapes=[
            pltpu.VMEM((width, chunk), jnp.bfloat16),
            pltpu.VMEM((width, share * width), jnp.bfloat16),
            pltpu.VMEM((chunk // 128, 8 * count, 128), jnp.float32),
            pltpu.VMEM((chunk // 128, 8 * count, 128), jnp.float32),
        ],
        cost_estimate=pl.CostEstimate(
            flops=2 * share * atoms * width * width * 8, bytes_accessed=20_000_000, transcendentals=0
        ),
        name="query_mix",
    )(table, coords, flat, weights_t, states)


def reduce_orders(bits):
    first = list(range(bits))
    second = list(first)
    if bits > 2:
        second[1], second[2] = second[2], second[1]
    return [first, second, first, second]


def piece_rows(rows, unit, pieces):
    units = rows // unit
    return [(units // pieces + (k < units % pieces)) * unit for k in range(pieces)]


def reduce_kernel(bits, local_ref, came_ref, out_ref, total, sent, landed, send_sems, recv_sems, gather_send, gather_recv):
    me = lax.axis_index("cell")

    def bit_of(b):
        return lax.rem(me // (1 << b), 2)

    def partner(b):
        return {"cell": me + (1 - 2 * bit_of(b)) * (1 << b)}

    barrier = pltpu.get_barrier_semaphore()
    for b in range(bits):
        pl.semaphore_signal(
            barrier, inc=1, device_id=partner(b), device_id_type=pl.DeviceIdType.MESH
        )
    orders = reduce_orders(bits)
    lengths = piece_rows(local_ref.shape[0], 16 * (1 << bits), len(orders))
    starts = [sum(lengths[:k]) for k in range(len(orders))]
    offsets = list(starts)

    def own(step, at):
        if step == 0:
            return local_ref[at, :] + came_ref[at, :].astype(jnp.float32)
        return total[at, :]

    pieces = range(len(orders))
    running = {}

    def copy_to(b, source, target, send_sem, recv_sem):
        copy = pltpu.make_async_remote_copy(
            src_ref=source,
            dst_ref=target,
            send_sem=send_sem,
            recv_sem=recv_sem,
            device_id=partner(b),
            device_id_type=pl.DeviceIdType.MESH,
        )
        copy.start()
        return copy

    def issue(k, stage):
        if stage < bits:
            b, half = orders[k][stage], lengths[k] // 2
            away = pl.multiple_of(starts[k] + (1 - bit_of(b)) * half, 16)
            at = pl.ds(offsets[k], half)
            sent[at, :] = own(stage, pl.ds(away, half)).astype(jnp.bfloat16)
            if stage == 0 and k == 0:
                pl.semaphore_wait(barrier, bits)
            running[k, stage] = copy_to(
                b, sent.at[at, :], landed.at[at, :], send_sems.at[k, stage], recv_sems.at[k, stage]
            )
        else:
            step = 2 * bits - 1 - stage
            at = pl.ds(pl.multiple_of(starts[k], 16), lengths[k])
            running[k, stage] = copy_to(
                orders[k][step], out_ref.at[at, :], out_ref.at[at, :],
                gather_send.at[k, step], gather_recv.at[k, step],
            )

    def finish(k, stage):
        running[k, stage].wait_recv()
        if stage < bits:
            half = lengths[k] // 2
            keep = pl.multiple_of(starts[k] + bit_of(orders[k][stage]) * half, 16)
            at = pl.ds(offsets[k], half)
            summed = own(stage, pl.ds(keep, half)) + landed[at, :].astype(jnp.float32)
            if stage == bits - 1:
                out_ref[pl.ds(keep, half), :] = summed.astype(jnp.bfloat16)
            else:
                total[pl.ds(keep, half), :] = summed
            starts[k], lengths[k] = keep, half
            offsets[k] += half
        else:
            step = 2 * bits - 1 - stage
            starts[k] = starts[k] - bit_of(orders[k][step]) * lengths[k]
            lengths[k] = 2 * lengths[k]

    for stage in range(2 * bits + 1):
        for k in pieces:
            if stage > 0:
                finish(k, stage - 1)
            if stage < 2 * bits:
                issue(k, stage)
    for copy in running.values():
        copy.wait_send()


def reduce_states(local, came, cells):
    bits = cells.bit_length() - 1
    rows, width = local.shape
    pieces = len(reduce_orders(bits))
    return pl.pallas_call(
        functools.partial(reduce_kernel, bits),
        out_shape=jax.ShapeDtypeStruct((rows, width), jnp.bfloat16),
        in_specs=vmem(2),
        out_specs=pl.BlockSpec(memory_space=pltpu.VMEM),
        scratch_shapes=[
            pltpu.VMEM((rows, width), jnp.float32),
            pltpu.VMEM((rows, width), jnp.bfloat16),
            pltpu.VMEM((rows, width), jnp.bfloat16),
        ]
        + [pltpu.SemaphoreType.DMA((pieces, bits))] * 4,
        compiler_params=pltpu.CompilerParams(collective_id=0, has_side_effects=True),
        cost_estimate=pl.CostEstimate(flops=20_000_000_000, bytes_accessed=60_000_000, transcendentals=0),
        name="reduce_states",
    )(local, came)


def radial_terms(own_positions, near_positions, near_features, filter_gains):
    differ = own_positions[:, None, :, :, None] - near_positions[:, :, :, None, :]
    distance = jnp.sqrt(jnp.sum(differ * differ, axis=2))
    centers = 2.0 + 2.0 * jnp.arange(filter_gains.shape[0], dtype=jnp.float32)
    scaled = (distance[:, :, None] - centers[None, None, :, None, None]) / radial_width
    radial = jnp.exp(-scaled * scaled).astype(jnp.bfloat16)
    summed = jnp.einsum(
        "gnkab,gnbf->gkaf", radial, near_features, preferred_element_type=jnp.float32
    )
    return jnp.sum(summed * filter_gains[None, :, None, :], axis=1)


def block_messages(live_count, group_width, picks, own_positions, extended_features, extended_positions, filter_gains):
    slot_count = picks.shape[0]
    initial = jnp.zeros(
        (slot_count, extended_features.shape[1], extended_features.shape[2]), jnp.float32
    )

    def block_advance(turn_index, running):
        at = turn_index * group_width
        picked = lax.dynamic_slice_in_dim(picks, at, group_width, 0)
        near_features = extended_features[picked]
        near_positions = extended_positions[picked]
        own = lax.dynamic_slice_in_dim(own_positions, at, group_width, 0)
        result = radial_terms(own, near_positions, near_features, filter_gains)
        return lax.dynamic_update_slice_in_dim(running, result, at, 0)

    group_total = (live_count + group_width - 1) // group_width
    return lax.fori_loop(0, group_total, block_advance, initial)


def join(features, places):
    padded = jnp.pad(places, ((0, 0), (0, 16 - places.shape[1]), (0, 0)))
    return jnp.concatenate([features, padded], axis=1)


def per_device(
    atom_features, positions, neighbours, counts, filter_gains, w_update, projections, w_output
):
    cells = lax.axis_size("cell")
    cell_index = lax.axis_index("cell")
    dirs_count = lax.axis_size("dir")
    dir_index = lax.axis_index("dir")
    capacity, block_atoms, width = atom_features.shape
    balanced_blocks = capacity // 2
    face_blocks = H
    faces = join(atom_features[:face_blocks], positions[:face_blocks])
    before = lax.ppermute(faces, "cell", [(i, (i + 1) % cells) for i in range(cells)])
    after = lax.ppermute(faces, "cell", [((i + 1) % cells, i) for i in range(cells)])
    float_positions = positions.astype(jnp.float32)
    extended_features = jnp.concatenate(
        [before[:, :block_atoms], atom_features, after[:, :block_atoms]], axis=0
    )
    axes = positions.shape[1]
    places_of = slice(block_atoms, block_atoms + axes)
    extended_positions = jnp.concatenate(
        [
            shift_component(before[:, places_of].astype(jnp.float32), -slab_width),
            float_positions,
            shift_component(after[:, places_of].astype(jnp.float32), slab_width),
        ],
        axis=0,
    )
    own_count = counts[cell_index]
    count_ends = jnp.cumsum(counts)
    first_live = (count_ends - counts)[cell_index]
    share_slots = capacity // dirs_count
    first_slot = (dir_index - first_live) % dirs_count

    def mine(array):
        dealt = array.reshape((share_slots, dirs_count) + array.shape[1:])
        return lax.dynamic_index_in_dim(dealt, first_slot, 1, keepdims=False)

    live_count = (own_count - first_slot + dirs_count - 1) // dirs_count
    own_features = mine(atom_features)
    own_places = mine(positions)
    own_float = own_places.astype(jnp.float32)
    message = block_messages(
        live_count, 2, mine(neighbours), own_float, extended_features, extended_positions, filter_gains
    )
    activated = jax.nn.silu(message).astype(jnp.bfloat16)
    updated = (
        own_features.astype(jnp.float32)
        + jnp.dot(activated, w_update, preferred_element_type=jnp.float32)
    ).astype(jnp.bfloat16)

    share = DIRS // dirs_count
    unit_rows = 16 * cells
    padded_rows = -(-share * width // unit_rows) * unit_rows
    tables = jnp.asarray(direction_rows(DIRS, dirs_count))
    weights_t = projections.T
    own_global = shift_component(own_float, slab_width * cell_index.astype(jnp.float32))
    own_coords = jnp.transpose(own_global, (1, 0, 2)).reshape(axes, -1)
    live_atoms = (live_count * block_atoms).astype(jnp.int32).reshape(1)

    def states_of(owner, dtype):
        part = lax.dynamic_index_in_dim(tables, owner, 0, keepdims=False)
        return kv_states(
            live_atoms, part, own_coords, updated.reshape(-1, width), weights_t, projections, share,
            padded_rows, dtype,
        )

    came = jnp.zeros((padded_rows, width), jnp.bfloat16)
    for hop in range(1, dirs_count):
        away = states_of((dir_index + hop) % dirs_count, jnp.bfloat16)
        arrived = lax.ppermute(away, "dir", [(i, (i + hop) % dirs_count) for i in range(dirs_count)])
        came = arrived if hop == 1 else came + arrived
    local_states = states_of(dir_index, jnp.float32)
    states = reduce_states(local_states, came, cells)

    slot_cap = max(1, 2 * balanced_blocks // cells)
    period = cells * slot_cap
    owner = jnp.arange(cells, dtype=jnp.int32)
    whole_rounds = slot_cap % dirs_count == 0
    per_owner = slot_cap // dirs_count if whole_rounds else slot_cap
    lane = jnp.arange(per_owner, dtype=jnp.int32)
    if whole_rounds:
        wanted = owner[:, None] * slot_cap + lane[None, :] * dirs_count + dir_index
    else:
        wanted = owner[:, None] * slot_cap + lane[None, :]
    offset = ((wanted - first_live) % period).reshape(-1)
    index = (offset - first_slot) // dirs_count
    is_mine = (offset < own_count) & ((offset - first_slot) % dirs_count == 0)
    picked = jnp.where(is_mine, index, 0)
    parcels = jnp.where(
        is_mine[:, None, None], join(updated, own_places)[picked], jnp.zeros((), jnp.bfloat16)
    )
    received = lax.all_to_all(parcels, "cell", split_axis=0, concat_axis=0, tiled=True)
    target = jnp.arange(balanced_blocks, dtype=jnp.int32)
    global_index = (target // slot_cap * cells + cell_index) * slot_cap + target % slot_cap
    source = jnp.sum((count_ends[None, :] <= global_index[:, None]).astype(jnp.int32), axis=1)
    if whole_rounds:
        def dealt_to(array, part):
            split = array.reshape((-1, dirs_count) + array.shape[1:])
            return lax.dynamic_index_in_dim(split, part, 1, keepdims=False)

        within = dealt_to(target % slot_cap, dir_index) // dirs_count
        rows = received[dealt_to(source, dir_index) * per_owner + within]
        gathered = [rows]
        for hop in range(1, dirs_count):
            gathered.append(
                lax.ppermute(rows, "dir", [(i, (i + hop) % dirs_count) for i in range(dirs_count)])
            )
        parts = jnp.stack(gathered, axis=1)
        order = (dir_index - jnp.arange(dirs_count, dtype=jnp.int32)) % dirs_count
        balanced = parts[:, order].reshape((balanced_blocks,) + parts.shape[2:])
    else:
        rows = received[source * per_owner + target % slot_cap]
        balanced = rows
        for hop in range(1, dirs_count):
            other = lax.ppermute(rows, "dir", [(i, (i + hop) % dirs_count) for i in range(dirs_count)])
            held = global_index % dirs_count == (dir_index - hop) % dirs_count
            balanced = jnp.where(held[:, None, None], other, balanced)
    balanced_features = balanced[:, :block_atoms]
    balanced_positions = shift_component(
        balanced[:, places_of].astype(jnp.float32),
        slab_width * source.astype(jnp.float32)[:, None, None],
    )
    share_blocks = balanced_blocks // dirs_count
    table = lax.dynamic_index_in_dim(tables, dir_index, 0, keepdims=False)

    def partial_mix(owner):
        features = lax.dynamic_slice_in_dim(balanced_features, owner * share_blocks, share_blocks, 0)
        places = lax.dynamic_slice_in_dim(balanced_positions, owner * share_blocks, share_blocks, 0)
        coords = jnp.transpose(places, (1, 0, 2)).reshape(axes, -1)
        return query_mix(table, coords, features.reshape(-1, width), weights_t, states, share)

    mixed_rows = None
    for hop in range(1, dirs_count):
        away = partial_mix((dir_index + hop) % dirs_count).astype(jnp.bfloat16)
        arrived = lax.ppermute(away, "dir", [(i, (i + hop) % dirs_count) for i in range(dirs_count)])
        arrived = arrived.astype(jnp.float32)
        mixed_rows = arrived if mixed_rows is None else mixed_rows + arrived
    kept = partial_mix(dir_index)
    mixed_rows = kept if mixed_rows is None else kept + mixed_rows
    mix_scale = 1.0 / math.sqrt(DIRS * cells * balanced_blocks * block_atoms * width)
    mixed = (mixed_rows * mix_scale).astype(jnp.bfloat16)
    attended = jnp.dot(mixed, w_output, preferred_element_type=jnp.float32).astype(jnp.bfloat16)
    return attended.reshape(-1, block_atoms, width)


def solution(mesh):
    placed = (
        P("cell", None, None),
        P("cell", None, None),
        P("cell", None),
        P(),
        P(),
        P(),
        P(),
        P(),
    )
    return jax.shard_map(
        per_device,
        mesh=mesh,
        in_specs=placed,
        out_specs=P(("cell", "dir"), None, None),
        check_vma=False,
    )
```

```python
import functools
import math

import jax
import jax.numpy as jnp
import numpy as np
from jax import lax
from jax.experimental import pallas as pl
from jax.experimental.pallas import tpu as pltpu
from jax.sharding import PartitionSpec as P

DIRS = 50
H = 4


slab_width = 12.0
radial_width = 0.6
golden_turn = math.pi * (3.0 - math.sqrt(5.0))


def shift_component(positions_in, amount):
    marker = (jnp.arange(positions_in.shape[-2]) == 0).astype(jnp.float32)
    return positions_in + amount * marker[:, None]


def direction_rows(total, shares):
    order = np.arange(total, dtype=np.float64)
    height = 1.0 - (2.0 * order + 1.0) / total
    radius = np.sqrt(1.0 - height * height)
    turning = order * golden_turn
    share = total // shares
    table = np.zeros((shares, -(-share // 8) * 8, 128), np.float32)
    unit = np.stack([radius * np.cos(turning), radius * np.sin(turning), height], axis=1)
    table[:, :share, :3] = unit.reshape(shares, share, 3)
    return table


def directions_per_turn(share):
    return max(g for g in range(1, 6) if share % g == 0)


def store_powers(table, coords, half, cosines, sines):
    base = (
        table[:, 0:1] * coords[0:1] + table[:, 1:2] * coords[1:2] + table[:, 2:3] * coords[2:3]
    ) * (0.5 / half)
    count = table.shape[0]
    c1, s1 = jnp.cos(base), jnp.sin(base)
    powers = {1: (c1, s1)}
    for n in range(2, 9):
        (ca, sa), (cb, sb) = powers[n // 2], powers[n - n // 2]
        powers[n] = (ca * cb - sa * sb, sa * cb + ca * sb)
    for n in range(1, 9):
        for tile in range(base.shape[1] // 128):
            lanes = slice(tile * 128, (tile + 1) * 128)
            cosines[tile, (n - 1) * count : n * count, :] = powers[n][0][:, lanes]
            sines[tile, (n - 1) * count : n * count, :] = powers[n][1][:, lanes]


def rotated(features, direction, count, half, cosines, sines):
    rows = pl.ds(direction, 8, stride=count)
    last = pl.ds(7 * count + direction, 1)

    def across(held, at):
        return jnp.concatenate([held[tile, at, :] for tile in range(held.shape[0])], axis=1)

    cosine, sine = across(cosines, rows), across(sines, rows)
    step_c = jnp.broadcast_to(across(cosines, last), cosine.shape)
    step_s = jnp.broadcast_to(across(sines, last), sine.shape)
    double = 2.0 * step_c
    older = None
    turned = []
    for first in range(0, half, 8):
        if first == 8:
            older = (cosine, sine)
            cosine, sine = cosine * step_c - sine * step_s, sine * step_c + cosine * step_s
        elif first > 8:
            held = (cosine, sine)
            cosine, sine = double * cosine - older[0], double * sine - older[1]
            older = held
        turned.append((cosine, sine))
    low, high = [], []
    for first in range(0, half, 16):
        pair = turned[first // 8 : first // 8 + 2]
        cosine, sine = [
            jnp.concatenate([both[which] for both in pair], axis=0).astype(jnp.bfloat16)
            for which in range(2)
        ]
        a = features[first : first + 16, :]
        b = features[half + first : half + first + 16, :]
        low.append(a * cosine - b * sine)
        high.append(b * cosine + a * sine)
    return [jnp.concatenate(low + high, axis=0)]


def kv_kernel(chunk, share, live_ref, table_ref, coords_ref, rows_ref, weights_t_ref, weights_ref, out_ref, states_ref, keys, cosines, sines):
    width = rows_ref.shape[1]
    half = width // 2
    count = table_ref.shape[0]
    per_turn = directions_per_turn(share)
    states_ref[...] = jnp.zeros_like(states_ref)
    live = live_ref[0]

    def advance(turn, carried):
        at = pl.ds(pl.multiple_of(turn * chunk, chunk), chunk)
        rows = rows_ref[at, :]
        keys[...] = lax.dot_general(
            weights_t_ref[width : 2 * width, :], rows, (((1,), (1,)), ((), ())),
            preferred_element_type=jnp.float32,
        ).astype(jnp.bfloat16)
        values = jnp.dot(rows, weights_ref[:, 2 * width :], preferred_element_type=jnp.float32)
        index = turn * chunk + lax.broadcasted_iota(jnp.int32, values.shape, 0)
        values = jnp.where(index < live, values, 0.0).astype(jnp.bfloat16)
        store_powers(table_ref[...], coords_ref[:, at], half, cosines, sines)

        for group in range(share // per_turn):
            parts = []
            for j in range(per_turn):
                parts += rotated(keys, group * per_turn + j, count, half, cosines, sines)
            size = per_turn * width
            states_ref[group * size : (group + 1) * size, :] += jnp.dot(
                jnp.concatenate(parts, axis=0), values, preferred_element_type=jnp.float32
            )
        return carried

    lax.fori_loop(0, (live + chunk - 1) // chunk, advance, 0)
    out_ref[...] = states_ref[...].astype(out_ref.dtype)


def query_kernel(chunk, share, table_ref, coords_ref, rows_ref, weights_t_ref, states_ref, out_ref, queries, flipped, cosines, sines):
    atoms, width = rows_ref.shape
    half = width // 2
    count = table_ref.shape[0]
    per_turn = directions_per_turn(share)
    for d in range(share):
        flipped[:, d * width : (d + 1) * width] = states_ref[d * width : (d + 1) * width, :].T

    def advance(turn, carried):
        at = pl.ds(pl.multiple_of(turn * chunk, chunk), chunk)
        queries[...] = lax.dot_general(
            weights_t_ref[:width, :], rows_ref[at, :], (((1,), (1,)), ((), ())),
            preferred_element_type=jnp.float32,
        ).astype(jnp.bfloat16)
        store_powers(table_ref[...], coords_ref[:, at], half, cosines, sines)
        summed = None
        for group in range(share // per_turn):
            parts = []
            for j in range(per_turn):
                parts += rotated(queries, group * per_turn + j, count, half, cosines, sines)
            size = per_turn * width
            term = jnp.dot(
                flipped[:, group * size : (group + 1) * size], jnp.concatenate(parts, axis=0),
                preferred_element_type=jnp.float32,
            )
            summed = term if summed is None else summed + term
        out_ref[at, :] = summed.T
        return carried

    lax.fori_loop(0, atoms // chunk, advance, 0)


def vmem(count):
    return [pl.BlockSpec(memory_space=pltpu.VMEM)] * count


def kv_states(live, table, coords, flat, weights_t, weights, share, padded_rows, dtype):
    width = flat.shape[1]
    chunk = 256
    count = table.shape[0]
    atoms = flat.shape[0] // 2
    return pl.pallas_call(
        functools.partial(kv_kernel, chunk, share),
        out_shape=jax.ShapeDtypeStruct((padded_rows, width), dtype),
        in_specs=[pl.BlockSpec(memory_space=pltpu.SMEM)] + vmem(5),
        out_specs=pl.BlockSpec(memory_space=pltpu.VMEM),
        scratch_shapes=[
            pltpu.VMEM((padded_rows, width), jnp.float32),
            pltpu.VMEM((width, chunk), jnp.bfloat16),
            pltpu.VMEM((chunk // 128, 8 * count, 128), jnp.float32),
            pltpu.VMEM((chunk // 128, 8 * count, 128), jnp.float32),
        ],
        cost_estimate=pl.CostEstimate(
            flops=2 * share * atoms * width * width * 8, bytes_accessed=20_000_000, transcendentals=0
        ),
        name="kv_states",
    )(live, table, coords, flat, weights_t, weights)


def query_mix(table, coords, flat, weights_t, states, share):
    atoms, width = flat.shape
    chunk = 256
    count = table.shape[0]
    return pl.pallas_call(
        functools.partial(query_kernel, chunk, share),
        out_shape=jax.ShapeDtypeStruct((atoms, width), jnp.float32),
        in_specs=vmem(5),
        out_specs=pl.BlockSpec(memory_space=pltpu.VMEM),
        scratch_shapes=[
            pltpu.VMEM((width, chunk), jnp.bfloat16),
            pltpu.VMEM((width, share * width), jnp.bfloat16),
            pltpu.VMEM((chunk // 128, 8 * count, 128), jnp.float32),
            pltpu.VMEM((chunk // 128, 8 * count, 128), jnp.float32),
        ],
        cost_estimate=pl.CostEstimate(
            flops=2 * share * atoms * width * width * 8, bytes_accessed=20_000_000, transcendentals=0
        ),
        name="query_mix",
    )(table, coords, flat, weights_t, states)


def reduce_orders(bits):
    first = list(range(bits))
    second = list(first)
    if bits > 2:
        second[1], second[2] = second[2], second[1]
    return [first, second, first, second]


def piece_rows(rows, unit, pieces):
    units = rows // unit
    return [(units // pieces + (k < units % pieces)) * unit for k in range(pieces)]


def reduce_kernel(bits, local_ref, away_ref, out_ref, total, sent, landed, turned, crossed, arrived, send_sems, recv_sems, gather_send, gather_recv, cross_send, cross_recv):
    me = lax.axis_index("cell")

    def bit_of(b):
        return lax.rem(me // (1 << b), 2)

    def partner(b):
        return {"cell": me + (1 - 2 * bit_of(b)) * (1 << b)}

    barrier = pltpu.get_barrier_semaphore()
    for b in range(bits):
        pl.semaphore_signal(
            barrier, inc=1, device_id=partner(b), device_id_type=pl.DeviceIdType.MESH
        )
    other = {"dir": 1 - lax.axis_index("dir")}
    pl.semaphore_signal(barrier, inc=1, device_id=other, device_id_type=pl.DeviceIdType.MESH)
    orders = reduce_orders(bits)
    lengths = piece_rows(local_ref.shape[0], 16 * (1 << bits), len(orders))
    starts = [sum(lengths[:k]) for k in range(len(orders))]
    offsets = list(starts)

    def own(step, at):
        return local_ref[at, :] if step == 0 else total[at, :]

    pieces = range(len(orders))
    running = {}

    def copy_to(device, source, target, send_sem, recv_sem):
        copy = pltpu.make_async_remote_copy(
            src_ref=source,
            dst_ref=target,
            send_sem=send_sem,
            recv_sem=recv_sem,
            device_id=device,
            device_id_type=pl.DeviceIdType.MESH,
        )
        copy.start()
        return copy

    def issue(k, stage):
        if stage < bits:
            b, half = orders[k][stage], lengths[k] // 2
            away = pl.multiple_of(starts[k] + (1 - bit_of(b)) * half, 16)
            at = pl.ds(offsets[k], half)
            sent[at, :] = own(stage, pl.ds(away, half)).astype(jnp.bfloat16)
            if stage == 0 and k == 0:
                pl.semaphore_wait(barrier, bits + 1)
            if stage == 0:
                turned[at, :] = away_ref[pl.ds(away, half), :]
                running[k, "turned"] = copy_to(
                    partner(b), turned.at[at, :], crossed.at[at, :], cross_send.at[k, 0], cross_recv.at[k, 0]
                )
            running[k, stage] = copy_to(
                partner(b), sent.at[at, :], landed.at[at, :], send_sems.at[k, stage], recv_sems.at[k, stage]
            )
        else:
            step = 2 * bits - 1 - stage
            at = pl.ds(pl.multiple_of(starts[k], 16), lengths[k])
            running[k, stage] = copy_to(
                partner(orders[k][step]), out_ref.at[at, :], out_ref.at[at, :],
                gather_send.at[k, step], gather_recv.at[k, step],
            )

    def finish(k, stage):
        running[k, stage].wait_recv()
        if stage < bits:
            half = lengths[k] // 2
            keep = pl.multiple_of(starts[k] + bit_of(orders[k][stage]) * half, 16)
            at = pl.ds(offsets[k], half)
            summed = own(stage, pl.ds(keep, half)) + landed[at, :].astype(jnp.float32)
            if stage == bits - 1:
                out_ref[pl.ds(keep, half), :] = summed.astype(jnp.bfloat16)
            else:
                total[pl.ds(keep, half), :] = summed
            if stage == 0:
                running[k, "turned"].wait_recv()
                rest = pl.ds(offsets[k] + half, half)
                turned[rest, :] = (
                    away_ref[pl.ds(keep, half), :].astype(jnp.float32) + crossed[at, :].astype(jnp.float32)
                ).astype(jnp.bfloat16)
                running[k, "across"] = copy_to(
                    other, turned.at[rest, :], arrived.at[rest, :], cross_send.at[k, 1], cross_recv.at[k, 1]
                )
            starts[k], lengths[k] = keep, half
            offsets[k] += half
        else:
            step = 2 * bits - 1 - stage
            starts[k] = starts[k] - bit_of(orders[k][step]) * lengths[k]
            lengths[k] = 2 * lengths[k]

    def absorb(k):
        running[k, "across"].wait_recv()
        held = pl.ds(pl.multiple_of(starts[k], 16), lengths[k])
        came = arrived[pl.ds(offsets[k], lengths[k]), :]
        total[held, :] = total[held, :] + came.astype(jnp.float32)

    for k in pieces:
        issue(k, 0)
    for k in pieces:
        finish(k, 0)
    for stage in range(1, 2 * bits + 1):
        for k in pieces:
            if stage == 1:
                absorb(k)
            else:
                finish(k, stage - 1)
            if stage < 2 * bits:
                issue(k, stage)
    for copy in running.values():
        copy.wait_send()


def reduce_states(local, away, cells):
    bits = cells.bit_length() - 1
    rows, width = local.shape
    pieces = len(reduce_orders(bits))
    return pl.pallas_call(
        functools.partial(reduce_kernel, bits),
        out_shape=jax.ShapeDtypeStruct((rows, width), jnp.bfloat16),
        in_specs=vmem(2),
        out_specs=pl.BlockSpec(memory_space=pltpu.VMEM),
        scratch_shapes=[
            pltpu.VMEM((rows, width), jnp.float32),
        ]
        + [pltpu.VMEM((rows, width), jnp.bfloat16)] * 5
        + [pltpu.SemaphoreType.DMA((pieces, bits))] * 4
        + [pltpu.SemaphoreType.DMA((pieces, 2))] * 2,
        compiler_params=pltpu.CompilerParams(collective_id=0, has_side_effects=True),
        cost_estimate=pl.CostEstimate(flops=20_000_000_000, bytes_accessed=60_000_000, transcendentals=0),
        name="reduce_states",
    )(local, away)


def radial_terms(own_positions, near_positions, near_features, filter_gains):
    differ = own_positions[:, None, :, :, None] - near_positions[:, :, :, None, :]
    distance = jnp.sqrt(jnp.sum(differ * differ, axis=2))
    centers = 2.0 + 2.0 * jnp.arange(filter_gains.shape[0], dtype=jnp.float32)
    scaled = (distance[:, :, None] - centers[None, None, :, None, None]) / radial_width
    radial = jnp.exp(-scaled * scaled).astype(jnp.bfloat16)
    summed = jnp.einsum(
        "gnkab,gnbf->gkaf", radial, near_features, preferred_element_type=jnp.float32
    )
    return jnp.sum(summed * filter_gains[None, :, None, :], axis=1)


def block_messages(live_count, group_width, picks, own_positions, extended_features, extended_positions, filter_gains):
    slot_count = picks.shape[0]
    initial = jnp.zeros(
        (slot_count, extended_features.shape[1], extended_features.shape[2]), jnp.float32
    )

    def block_advance(turn_index, running):
        at = turn_index * group_width
        picked = lax.dynamic_slice_in_dim(picks, at, group_width, 0)
        near_features = extended_features[picked]
        near_positions = extended_positions[picked]
        own = lax.dynamic_slice_in_dim(own_positions, at, group_width, 0)
        result = radial_terms(own, near_positions, near_features, filter_gains)
        return lax.dynamic_update_slice_in_dim(running, result, at, 0)

    group_total = (live_count + group_width - 1) // group_width
    return lax.fori_loop(0, group_total, block_advance, initial)


def join(features, places):
    padded = jnp.pad(places, ((0, 0), (0, 16 - places.shape[1]), (0, 0)))
    return jnp.concatenate([features, padded], axis=1)


def per_device(
    atom_features, positions, neighbours, counts, filter_gains, w_update, projections, w_output
):
    cells = lax.axis_size("cell")
    cell_index = lax.axis_index("cell")
    dirs_count = lax.axis_size("dir")
    dir_index = lax.axis_index("dir")
    capacity, block_atoms, width = atom_features.shape
    balanced_blocks = capacity // 2
    face_blocks = H
    faces = join(atom_features[:face_blocks], positions[:face_blocks])
    before = lax.ppermute(faces, "cell", [(i, (i + 1) % cells) for i in range(cells)])
    after = lax.ppermute(faces, "cell", [((i + 1) % cells, i) for i in range(cells)])
    float_positions = positions.astype(jnp.float32)
    extended_features = jnp.concatenate(
        [before[:, :block_atoms], atom_features, after[:, :block_atoms]], axis=0
    )
    axes = positions.shape[1]
    places_of = slice(block_atoms, block_atoms + axes)
    extended_positions = jnp.concatenate(
        [
            shift_component(before[:, places_of].astype(jnp.float32), -slab_width),
            float_positions,
            shift_component(after[:, places_of].astype(jnp.float32), slab_width),
        ],
        axis=0,
    )
    cell_order = jnp.arange(cells, dtype=jnp.int32)
    own_count = jnp.sum(jnp.where(cell_order == cell_index, counts, 0))
    first_live = jnp.sum(jnp.where(cell_order < cell_index, counts, 0))
    count_ends = jnp.cumsum(counts)
    share_slots = capacity // dirs_count
    first_slot = (dir_index - first_live) % dirs_count

    def mine(array):
        dealt = array.reshape((share_slots, dirs_count) + array.shape[1:])
        return lax.dynamic_index_in_dim(dealt, first_slot, 1, keepdims=False)

    live_count = (own_count - first_slot + dirs_count - 1) // dirs_count
    own_features = mine(atom_features)
    own_places = mine(positions)
    own_float = own_places.astype(jnp.float32)
    message = block_messages(
        live_count, 2, mine(neighbours), own_float, extended_features, extended_positions, filter_gains
    )
    activated = jax.nn.silu(message).astype(jnp.bfloat16)
    updated = (
        own_features.astype(jnp.float32)
        + jnp.dot(activated, w_update, preferred_element_type=jnp.float32)
    ).astype(jnp.bfloat16)

    share = DIRS // dirs_count
    unit_rows = 16 * cells
    padded_rows = -(-share * width // unit_rows) * unit_rows
    tables = jnp.asarray(direction_rows(DIRS, dirs_count))
    weights_t = projections.T
    own_global = shift_component(own_float, slab_width * cell_index.astype(jnp.float32))
    own_coords = jnp.transpose(own_global, (1, 0, 2)).reshape(axes, -1)
    live_atoms = (live_count * block_atoms).astype(jnp.int32).reshape(1)

    def states_of(owner, dtype):
        part = lax.dynamic_index_in_dim(tables, owner, 0, keepdims=False)
        return kv_states(
            live_atoms, part, own_coords, updated.reshape(-1, width), weights_t, projections, share,
            padded_rows, dtype,
        )

    away_states = states_of((dir_index + 1) % dirs_count, jnp.bfloat16)
    local_states = states_of(dir_index, jnp.float32)
    states = reduce_states(local_states, away_states, cells)

    slot_cap = max(1, 2 * balanced_blocks // cells)
    period = cells * slot_cap
    owner = jnp.arange(cells, dtype=jnp.int32)
    whole_rounds = slot_cap % dirs_count == 0
    per_owner = slot_cap // dirs_count if whole_rounds else slot_cap
    lane = jnp.arange(per_owner, dtype=jnp.int32)
    if whole_rounds:
        wanted = owner[:, None] * slot_cap + lane[None, :] * dirs_count + dir_index
    else:
        wanted = owner[:, None] * slot_cap + lane[None, :]
    offset = ((wanted - first_live) % period).reshape(-1)
    index = (offset - first_slot) // dirs_count
    is_mine = (offset < own_count) & ((offset - first_slot) % dirs_count == 0)
    picked = jnp.where(is_mine, index, 0)
    parcels = jnp.where(
        is_mine[:, None, None], join(updated, own_places)[picked], jnp.zeros((), jnp.bfloat16)
    )
    received = lax.all_to_all(parcels, "cell", split_axis=0, concat_axis=0, tiled=True)
    target = jnp.arange(balanced_blocks, dtype=jnp.int32)
    global_index = (target // slot_cap * cells + cell_index) * slot_cap + target % slot_cap
    source = jnp.sum((count_ends[None, :] <= global_index[:, None]).astype(jnp.int32), axis=1)
    if whole_rounds:
        def dealt_to(array, part):
            split = array.reshape((-1, dirs_count) + array.shape[1:])
            return lax.dynamic_index_in_dim(split, part, 1, keepdims=False)

        within = dealt_to(target % slot_cap, dir_index) // dirs_count
        rows = received[dealt_to(source, dir_index) * per_owner + within]
        gathered = [rows]
        for hop in range(1, dirs_count):
            gathered.append(
                lax.ppermute(rows, "dir", [(i, (i + hop) % dirs_count) for i in range(dirs_count)])
            )
        parts = jnp.stack(gathered, axis=1)
        order = (dir_index - jnp.arange(dirs_count, dtype=jnp.int32)) % dirs_count
        balanced = parts[:, order].reshape((balanced_blocks,) + parts.shape[2:])
    else:
        rows = received[source * per_owner + target % slot_cap]
        balanced = rows
        for hop in range(1, dirs_count):
            other = lax.ppermute(rows, "dir", [(i, (i + hop) % dirs_count) for i in range(dirs_count)])
            held = global_index % dirs_count == (dir_index - hop) % dirs_count
            balanced = jnp.where(held[:, None, None], other, balanced)
    balanced_features = balanced[:, :block_atoms]
    balanced_positions = shift_component(
        balanced[:, places_of].astype(jnp.float32),
        slab_width * source.astype(jnp.float32)[:, None, None],
    )
    share_blocks = balanced_blocks // dirs_count
    table = lax.dynamic_index_in_dim(tables, dir_index, 0, keepdims=False)

    def partial_mix(owner):
        features = lax.dynamic_slice_in_dim(balanced_features, owner * share_blocks, share_blocks, 0)
        places = lax.dynamic_slice_in_dim(balanced_positions, owner * share_blocks, share_blocks, 0)
        coords = jnp.transpose(places, (1, 0, 2)).reshape(axes, -1)
        return query_mix(table, coords, features.reshape(-1, width), weights_t, states, share)

    mixed_rows = None
    for hop in range(1, dirs_count):
        away = partial_mix((dir_index + hop) % dirs_count).astype(jnp.bfloat16)
        arrived = lax.ppermute(away, "dir", [(i, (i + hop) % dirs_count) for i in range(dirs_count)])
        arrived = arrived.astype(jnp.float32)
        mixed_rows = arrived if mixed_rows is None else mixed_rows + arrived
    kept = partial_mix(dir_index)
    mixed_rows = kept if mixed_rows is None else kept + mixed_rows
    mix_scale = 1.0 / math.sqrt(DIRS * cells * balanced_blocks * block_atoms * width)
    mixed = (mixed_rows * mix_scale).astype(jnp.bfloat16)
    attended = jnp.dot(mixed, w_output, preferred_element_type=jnp.float32).astype(jnp.bfloat16)
    return attended.reshape(-1, block_atoms, width)


def solution(mesh):
    placed = (
        P("cell", None, None),
        P("cell", None, None),
        P("cell", None),
        P(),
        P(),
        P(),
        P(),
        P(),
    )
    return jax.shard_map(
        per_device,
        mesh=mesh,
        in_specs=placed,
        out_specs=P(("cell", "dir"), None, None),
        check_vma=False,
    )
```
